512 devices in a mesh: dp: 16 (over y, core), seq: 32 (over z, x).
Axes of the slice: x: 4, y: 8, z: 8, core: 2. Of those that a mesh axis runs over, the one named last changes fastest.
Arguments:
- query_rows: bfloat16 [2048, 32, 2048], P('seq', 'dp'), may hold values from -6 to 6
- key_rows: bfloat16 [2048, 32, 2048], P('seq', 'dp'), may hold values from -6 to 6
- value_rows: bfloat16 [2048, 32, 2048], P('seq', 'dp'), may hold values from -6 to 6
- region_lengths: int32 [32], P('dp'), may hold values from 256 to 2048, as said below
- norm_gain: float32 [2048], replicated, may hold values from 0.1 to 1.9
- conv_weight: bfloat16 [9, 128, 128], replicated, may hold values from -0.1875 to 0.1875
- cotangent: bfloat16 [32, 128, 256, 128], P('dp', 'seq'), may hold values from -6 to 6
Outputs:
- decoded: bfloat16 [32, 128, 256, 128], P('dp', 'seq')
- weight_grad: float32 [9, 128, 128], replicated
The draws below stay inside these ranges and needn't reach their ends.
Inputs may be any that keep to these rules, and one draw needn't show every extreme that they name: Region r's tokens fill its first region_lengths[r] slots; in every draw some region fills all 2048 slots.
All inputs are finite; a program needn't handle non-finite values.
Results may differ from the reference program's by a relative error of at most 0.0063.
Values may be sent and summed in bfloat16 or wider, within the bound.
A program may use at most 64 MiB of HBM per device.

```python
import math
import jax
import jax.numpy as jnp
from jax import lax

D = 2048
HEADS = 16
PATCH = 4
TOK_DEV = 64
HD = 128
CH = 128
CAP = 2048
REGIONS = 32
ROWS_PIX = 128
COLS_PIX = 256
N_SEQ = 32


def paired_rows(key):
    whole_shape = (CAP, REGIONS, D)
    query_vals = jnp.clip(jax.random.normal(jax.random.fold_in(key, 11), whole_shape, jnp.float32), -6.0, 6.0)
    key_vals = jnp.clip(jax.random.normal(jax.random.fold_in(key, 12), whole_shape, jnp.float32), -6.0, 6.0)
    return (query_vals, key_vals)


def draw_query_rows(key, part):
    return paired_rows(key)[0].astype(jnp.bfloat16)


def draw_key_rows(key, part):
    return paired_rows(key)[1].astype(jnp.bfloat16)


def draw_region_lengths(key, part):
    values = jax.random.randint(jax.random.fold_in(key, 21), (REGIONS,), CAP // 8, CAP + 1)
    longest = jax.random.randint(jax.random.fold_in(key, 22), (), 0, REGIONS)
    return jnp.where(jnp.arange(REGIONS) == longest, CAP, values).astype(jnp.int32)


def block_scale(own_key, shape, cuts, least, high):
    gain, own = 1.0, jax.random.fold_in(own_key, 6)
    for dim, shards_of in cuts:
        heights = jnp.exp(jax.random.uniform(jax.random.fold_in(own, dim), (shards_of,), jnp.float32, least / len(cuts), high / len(cuts)))
        gain = gain * jnp.repeat(heights, shape[dim] // shards_of).reshape([-1 if axis == dim else 1 for axis in range(len(shape))])
    return gain


def bell_draw(own_key, extent, spread, most, split=(), held_as=jnp.bfloat16):
    entries = jax.random.normal(own_key, extent, jnp.float32) * spread
    if len(split) > 0:
        entries = block_scale(own_key, extent, split, -0.22, 0.18) * entries
    return jnp.clip(entries, min=-most, max=most).astype(held_as)


def setup_inputs(seed: int = 0) -> dict:
    key_of = jax.random.split(jax.random.key(seed), 8)
    return {
        "query_rows": draw_query_rows(jax.random.fold_in(key_of[7], 71), 0),
        "key_rows": draw_key_rows(jax.random.fold_in(key_of[7], 71), 0),
        "value_rows": bell_draw(key_of[2], (CAP, REGIONS, D), 1.0, 6.0, ((0, 32), (1, 16))),
        "region_lengths": draw_region_lengths(jax.random.fold_in(key_of[7], 71), 0),
        "norm_gain": jnp.clip(1.0 + 0.18 * jax.random.normal(key_of[4], (D,), jnp.float32), 0.1, 1.9),
        "conv_weight": bell_draw(key_of[5], (9, CH, CH), (9 * CH) ** -0.5, 0.1875),
        "cotangent": bell_draw(key_of[6], (REGIONS, ROWS_PIX, COLS_PIX, CH), 1.0, 6.0, ((0, 16), (1, 32))),
    }


def attend_one(packed):
    query_mat, key_mat, value_mat, key_count = packed
    scores = jnp.dot(query_mat, key_mat.T, preferred_element_type=jnp.float32) * (1.0 / math.sqrt(HD))
    key_valid = jnp.arange(CAP, dtype=jnp.int32) < key_count
    scores = jnp.where(key_valid[None, :], scores, -1e+30)
    top_score = lax.optimization_barrier(jnp.max(scores, axis=1, keepdims=True))
    powers = jnp.exp(scores - top_score)
    totals = lax.optimization_barrier(jnp.sum(powers, axis=1, keepdims=True))
    mixed = jnp.dot(powers.astype(jnp.bfloat16), value_mat, preferred_element_type=jnp.float32) / totals
    return mixed.astype(jnp.bfloat16)

def reference(query_rows, key_rows, value_rows, region_lengths, norm_gain, conv_weight, cotangent):
    item_total = REGIONS * HEADS

    def heads_major(source):
        return source.reshape(CAP, item_total, HD).transpose(1, 0, 2)
    counts = jnp.repeat(region_lengths, HEADS)
    attended = lax.map(attend_one, (heads_major(query_rows), heads_major(key_rows), heads_major(value_rows), counts))
    attended = attended.transpose(1, 0, 2).reshape(CAP, REGIONS, D)
    values32 = attended.astype(jnp.float32)
    mean_val = lax.optimization_barrier(jnp.mean(values32, axis=-1, keepdims=True))
    centered = values32 - mean_val
    variance = lax.optimization_barrier(jnp.mean(centered * centered, axis=-1, keepdims=True))
    normed = centered * lax.rsqrt(variance + 1e-05) * norm_gain
    positions = jnp.arange(CAP, dtype=jnp.int32)
    token_live = positions[:, None] < region_lengths[None, :]
    normed = jnp.where(token_live[:, :, None], normed, 0.0).astype(jnp.bfloat16)
    image = normed.reshape(N_SEQ, TOK_DEV, REGIONS, PATCH, PATCH, CH).transpose(2, 0, 3, 1, 4, 5)
    image = image.reshape(REGIONS, ROWS_PIX, COLS_PIX, CH)
    padded = jnp.pad(image, ((0, 0), (1, 1), (1, 1), (0, 0)))
    cot_flat = cotangent.reshape(-1, CH)
    accum = jnp.zeros((REGIONS * ROWS_PIX * COLS_PIX, CH), jnp.float32)
    grads = []
    for tap_number in range(9):
        row_shift, col_shift = divmod(tap_number, 3)
        window = padded[:, row_shift:row_shift + ROWS_PIX, col_shift:col_shift + COLS_PIX, :].reshape(-1, CH)
        accum = accum + jnp.dot(window, conv_weight[tap_number], preferred_element_type=jnp.float32)
        grads.append(jnp.dot(window.T, cot_flat, preferred_element_type=jnp.float32))
    decoded = accum.reshape(REGIONS, ROWS_PIX, COLS_PIX, CH).astype(jnp.bfloat16)
    factor = 1.0 / math.sqrt(PATCH * COLS_PIX)
    weight_grad = jnp.stack(grads) * factor
    return (decoded, weight_grad)
```

```python
import functools
import math

import jax
import jax.numpy as jnp
from jax import lax
from jax.experimental import pallas as pl
from jax.experimental.pallas import tpu as pltpu
from jax.sharding import PartitionSpec as P

HEADS = 16
PATCH = 4
MESH = pl.DeviceIdType.MESH
X = 4
OWNED = 18


def reduce_kernel(n_dp, n_seq, g_ref, out_ref, buf1, acc1, buf2, acc2, buf3, fin,
                  s1, r1, s2, r2, s3, r3, s4, r4, s5, r5, s6, r6):
    dp, seq = lax.axis_index("dp"), lax.axis_index("seq")
    n_z = n_seq // X
    n_yz = (n_dp // 2) * n_z
    core, x = dp % 2, seq % X
    member = (dp // 2) * n_z + seq // X
    partner = (dp + 1 - 2 * core, seq)

    def x_peer(step):
        return (dp, seq - x + (x + step) % X)

    def yz_device(index):
        return ((index // n_z) * 2 + core, (index % n_z) * X + x)

    barrier = pltpu.get_barrier_semaphore()
    pl.semaphore_signal(barrier, inc=1, device_id=partner, device_id_type=MESH)
    for step in range(1, X):
        pl.semaphore_signal(barrier, inc=1, device_id=x_peer(step), device_id_type=MESH)

    def greet(step, _):
        pl.semaphore_signal(barrier, inc=1, device_id=yz_device((member + step) % n_yz), device_id_type=MESH)
        return 0

    lax.fori_loop(1, n_yz, greet, 0)
    pl.semaphore_wait(barrier, 1 + (X - 1) + (n_yz - 1))

    def remote(src, dst, send, recv, device):
        return pltpu.make_async_remote_copy(src_ref=src, dst_ref=dst, send_sem=send, recv_sem=recv,
                                            device_id=device, device_id_type=MESH)

    swap = remote(g_ref.at[:, pl.ds(8 * (1 - core), 8)], buf1, s1, r1, partner)
    swap.start()
    swap.wait()
    acc1[...] = g_ref[:, pl.ds(8 * core, 8)] + buf1[...]
    copies = []
    for step in range(1, X):
        to = (x + step) % X
        copy = remote(acc1.at[:, pl.ds(2 * to, 2)], buf2.at[step - 1], s2.at[step - 1], r2.at[step - 1], x_peer(step))
        copy.start()
        copies.append(copy)
    for copy in copies:
        copy.wait()
    acc2[...] = (acc1[:, pl.ds(2 * x, 2)] + buf2[0]) + (buf2[1] + buf2[2])
    turned = (member + n_yz - core) % n_yz
    for tile in range(OWNED):
        owner = (3 * tile + core) % n_yz

        @pl.when(owner != member)
        def _():
            remote(acc2.at[tile // 2, tile % 2], buf3.at[member], s3, r3, yz_device(owner)).start()

    mine = turned // 3
    owns = jnp.logical_and(turned % 3 == 0, mine < OWNED)

    def wait_bytes(ref, sem):
        pltpu.make_async_copy(ref, ref, sem).wait()

    @pl.when(owns)
    def _():
        wait_bytes(buf3.at[pl.ds(0, OWNED - 1)], s3)
        wait_bytes(buf3.at[pl.ds(0, n_yz - 1)], r3)
        buf3[member] = acc2[mine // 2, mine % 2]
        fin[mine // 2, mine % 2] = jnp.sum(buf3[...], axis=0) * (1.0 / 32.0)
        part = fin.at[mine // 2, mine % 2]

        def spread(step, _):
            remote(part, part, s4, r4, yz_device((member + step) % n_yz)).start()
            return 0

        lax.fori_loop(1, n_yz, spread, 0)
        wait_bytes(buf3.at[pl.ds(0, n_yz - 1)], s4)
        wait_bytes(buf3.at[pl.ds(0, OWNED - 1)], r4)

    @pl.when(jnp.logical_not(owns))
    def _():
        wait_bytes(buf3.at[pl.ds(0, OWNED)], s3)
        wait_bytes(buf3.at[pl.ds(0, OWNED)], r4)

    def place(which):
        return out_ref.at[:, pl.ds(8 * core + 2 * which, 2)]

    copies = []
    for step in range(1, X):
        copy = remote(fin, place(x), s5.at[step - 1], r5.at[step - 1], x_peer(step))
        copy.start()
        copies.append(copy)
    out_ref[:, pl.ds(8 * core + 2 * x, 2)] = fin[...]
    forwards = [remote(fin, place(x), s6.at[0], r6.at[0], partner)]
    forwards[0].start()
    for step in range(1, X):
        copies[step - 1].wait()
        came = place((x + X - step) % X)
        forward = remote(came, came, s6.at[step], r6.at[step], partner)
        forward.start()
        forwards.append(forward)
    for forward in forwards:
        forward.wait()


def all_sum(grads, n_dp, n_seq):
    f32 = jnp.float32
    n_yz = (n_dp // 2) * (n_seq // X)
    dma = pltpu.SemaphoreType.DMA
    out = pl.pallas_call(
        functools.partial(reduce_kernel, n_dp, n_seq),
        out_shape=jax.ShapeDtypeStruct((9, 16, 8, 128), f32),
        in_specs=[pl.BlockSpec(memory_space=pltpu.VMEM)],
        out_specs=pl.BlockSpec(memory_space=pltpu.VMEM),
        scratch_shapes=[
            pltpu.VMEM((9, 8, 8, 128), f32), pltpu.VMEM((9, 8, 8, 128), f32),
            pltpu.VMEM((3, 9, 2, 8, 128), f32), pltpu.VMEM((9, 2, 8, 128), f32),
            pltpu.VMEM((n_yz, 8, 128), f32), pltpu.VMEM((9, 2, 8, 128), f32),
            dma, dma, dma((3,)), dma((3,)), dma, dma, dma, dma, dma((3,)), dma((3,)), dma((4,)), dma((4,)),
        ],
        compiler_params=pltpu.CompilerParams(collective_id=0, has_side_effects=True),
        name="reduce_all",
    )(grads.reshape(9, 16, 8, 128))
    return out.reshape(9, 128, 128)


def extended(shard, sides, width):
    for axis, dim in sides:
        size, length = (lax.axis_size(axis), shard.shape[dim])
        up = [(i, (i + 1) % size) for i in range(size - 1)]
        down = [(j, i) for i, j in up]
        last = lax.slice_in_dim(shard, length - width, length, axis=dim)
        initial = lax.slice_in_dim(shard, 0, width, axis=dim)
        before = lax.ppermute(last, axis, up)
        after = lax.ppermute(initial, axis, down)
        shard = jnp.concatenate([before, shard, after], axis=dim)
    return shard


def attend(query_mat, key_mat, value_mat, live_rows, key_count):
    total_rows = query_mat.shape[0]
    block_rows = min(512, total_rows)
    scale_factor = 1.0 / math.sqrt(query_mat.shape[1])
    key_valid = jnp.arange(key_mat.shape[0], dtype=jnp.int32) < key_count

    def one_block(number, output):
        start_row = number * block_rows
        query_blk = lax.dynamic_slice_in_dim(query_mat, start_row, block_rows, 0)
        scores = (
            lax.dot_general(
                query_blk, key_mat, (((1,), (1,)), ((), ())), preferred_element_type=jnp.float32
            )
            * scale_factor
        )
        scores = jnp.where(key_valid[None, :], scores, -1e30)
        top_score = jnp.max(scores, axis=1, keepdims=True)
        powers = jnp.exp(scores - top_score)
        totals = jnp.sum(powers, axis=1, keepdims=True)
        mixed = (
            jnp.dot(powers.astype(jnp.bfloat16), value_mat, preferred_element_type=jnp.float32)
            / totals
        )
        return lax.dynamic_update_slice_in_dim(output, mixed.astype(jnp.bfloat16), start_row, 0)

    blocks_live = (live_rows + block_rows - 1) // block_rows
    return lax.fori_loop(0, blocks_live, one_block, jnp.zeros(query_mat.shape, jnp.bfloat16))


def pick_length(lengths_local, which):
    return jnp.sum(
        jnp.where(jnp.arange(lengths_local.shape[0], dtype=jnp.int32) == which, lengths_local, 0)
    )


def body(query_rows, key_rows, value_rows, region_lengths, norm_gain, conv_weight, cotangent):
    local_tokens, group_regions, model_width = query_rows.shape
    head_width = model_width // HEADS
    seq_count = lax.axis_size("seq")
    seq_index = lax.axis_index("seq")
    item_total = group_regions * HEADS
    got_query, got_key, got_value = (
        lax.all_to_all(
            query_rows.reshape(local_tokens, item_total, head_width),
            "seq",
            split_axis=1,
            concat_axis=0,
            tiled=True,
        ),
        lax.all_to_all(
            key_rows.reshape(local_tokens, item_total, head_width),
            "seq",
            split_axis=1,
            concat_axis=0,
            tiled=True,
        ),
        lax.all_to_all(
            value_rows.reshape(local_tokens, item_total, head_width),
            "seq",
            split_axis=1,
            concat_axis=0,
            tiled=True,
        ),
    )
    per_device = item_total // seq_count
    global_item = seq_index * per_device + 0
    region_len = pick_length(region_lengths, global_item // HEADS)
    outputs = [attend(got_query[:, 0], got_key[:, 0], got_value[:, 0], region_len, region_len)]
    stacked = jnp.stack(outputs, axis=1)
    returned = lax.all_to_all(stacked, "seq", split_axis=0, concat_axis=1, tiled=True)
    attended = returned.reshape(local_tokens, group_regions, model_width)
    values32 = attended.astype(jnp.float32)
    mean_val = jnp.mean(values32, axis=-1, keepdims=True)
    centered = values32 - mean_val
    variance = jnp.mean(centered * centered, axis=-1, keepdims=True)
    normed = centered * lax.rsqrt(variance + 1e-05) * norm_gain
    positions = seq_index * local_tokens + jnp.arange(local_tokens, dtype=jnp.int32)
    token_live = positions[:, None] < region_lengths[None, :]
    normed = jnp.where(token_live[:, :, None], normed, 0.0).astype(jnp.bfloat16)
    channels = model_width // (PATCH * PATCH)
    pix_cols = local_tokens * PATCH
    image = normed.reshape(local_tokens, group_regions, PATCH, PATCH, channels).transpose(
        1, 2, 0, 3, 4
    )
    image = image.reshape(group_regions, PATCH, pix_cols, channels)
    rimmed = extended(image, (("seq", 1),), 1)
    padded = jnp.pad(rimmed, ((0, 0), (0, 0), (1, 1), (0, 0)))
    cot_flat = cotangent.reshape(-1, channels)
    accum = jnp.zeros((group_regions * PATCH * pix_cols, channels), jnp.float32)
    grads = []
    for tap_number in range(9):
        row_shift, col_shift = divmod(tap_number, 3)
        window = padded[
            :, row_shift : row_shift + PATCH, col_shift : col_shift + pix_cols, :
        ].reshape(-1, channels)
        accum = accum + jnp.dot(window, conv_weight[tap_number], preferred_element_type=jnp.float32)
        grads.append(jnp.dot(window.T, cot_flat, preferred_element_type=jnp.float32))
    decoded = accum.reshape(cotangent.shape).astype(jnp.bfloat16)
    local_grad = jnp.stack(grads)
    summed = all_sum(local_grad, lax.axis_size("dp"), seq_count)
    return (decoded, summed)


def solution(mesh):
    placed = (
        P("seq", "dp", None),
        P("seq", "dp", None),
        P("seq", "dp", None),
        P("dp"),
        P(),
        P(),
        P("dp", "seq", None, None),
    )
    return jax.shard_map(
        body,
        mesh=mesh,
        in_specs=placed,
        out_specs=(P("dp", "seq", None, None), P()),
        check_vma=False,
    )
```

```python
import functools
import math

import jax
import jax.numpy as jnp
from jax import lax
from jax.experimental import pallas as pl
from jax.experimental.pallas import tpu as pltpu
from jax.sharding import PartitionSpec as P

HEADS = 16
PATCH = 4
MESH = pl.DeviceIdType.MESH
X, Z = 4, 8
TOK, HD = 64, 128
OWNED = 18
F32, BF16 = jnp.float32, jnp.bfloat16


def remote(src, dst, send, recv, device):
    return pltpu.make_async_remote_copy(
        src_ref=src, dst_ref=dst, send_sem=send, recv_sem=recv, device_id=device, device_id_type=MESH
    )


def wait_bytes(ref, sem):
    pltpu.make_async_copy(ref, ref, sem).wait()


def step_kernel(n_dp, lens_ref, q_ref, k_ref, v_ref, gain_ref, w_ref, cot_ref, dec_ref, wg_ref,
                stage, rq, rk, rv, hold, probs, sums, o_mid, o_in, o_hold, att, ext, cot_t, grid, wide,
                grads, taps, buf1, acc1, buf2, acc2, buf3, fin,
                sx, rx, sz, rz, rr, so, ro, rro, sx2, rx2, sh, rh,
                s1, r1, s2, r2, s3, r3, s4, r4, s5, r5, s6, r6):
    dp, seq = lax.axis_index("dp"), lax.axis_index("seq")
    n_seq = X * Z
    n_yz = (n_dp // 2) * Z
    core, z, x = dp % 2, seq // X, seq % X
    member = (dp // 2) * Z + z
    partner = (dp + 1 - 2 * core, seq)
    half = 2 + 4 * core

    def x_device(step):
        return (dp, z * X + (x + step) % X)

    def z_device(step):
        return (dp, ((z + step) % Z) * X + x)

    def yz_device(index):
        return ((index // Z) * 2 + core, (index % Z) * X + x)

    barrier = pltpu.get_barrier_semaphore()

    def signal(device):
        pl.semaphore_signal(barrier, inc=1, device_id=device, device_id_type=MESH)

    def greet(step, _):
        signal(yz_device((member + step) % n_yz))
        return 0

    for step in range(1, X):
        signal(x_device(step))
    lax.fori_loop(1, n_yz, greet, 0)
    signal(partner)
    signal((dp, (seq + 1) % n_seq))
    signal((dp, (seq + n_seq - 1) % n_seq))
    pl.semaphore_wait(barrier, (X - 1) + (n_yz - 1) + 1 + 2)

    sources, landed = (q_ref, k_ref, v_ref), (rq, rk, rv)
    far_first = (4, 3, 5, 2, 6, 1, 7)

    x_copies = []
    for array in range(3):
        for step in (1, 3, 2):
            copy = remote(sources[array].at[:, (x + step) % X], stage.at[array, :, x],
                          sx.at[array, step - 1], rx.at[array, step - 1], x_device(step))
            copy.start()
            x_copies.append(copy)

    def along_z(array, blocks, column):
        for step in far_first:
            block = blocks.at[(z + step) % Z, column]
            if step == 4:
                remote(block, hold.at[array, column], sz.at[array], rr.at[array, column], z_device(half)).start()
            else:
                remote(block, landed[array].at[z, column], sz.at[array], rz.at[array], z_device(step)).start()

    def staged(array):
        for step in (1, 3, 2):
            column = (x + X - step) % X
            wait_bytes(stage.at[array, :, column], rx.at[array, step - 1])
            along_z(array, stage.at[array], column)
            landed[array][z, column] = stage[array, z, column]
        landed[array][z, x] = sources[array][z, x]

    def onward(array, column):
        wait_bytes(hold.at[array, column], rr.at[array, column])
        remote(hold.at[array, column], landed[array].at[(z + Z - half) % Z, column], sz.at[array], rz.at[array],
               z_device(half)).start()

    for array in range(3):
        along_z(array, sources[array], x)

    for row in range(PATCH):
        for region in range(2):
            grid[region] = cot_ref[region, row].astype(F32)
        for px in range(PATCH):
            part = [grid[region, pl.ds(px, TOK, stride=PATCH), :] for region in range(2)]
            cot_t[px * HD:(px + 1) * HD, row * 2 * TOK:(row + 1) * 2 * TOK] = jnp.concatenate(part).T.astype(BF16)
    wide[...] = jnp.zeros_like(wide)
    for dy in range(3):
        for dx in range(3):
            for px in range(PATCH):
                wide[dy, (px + dx) * HD:(px + dx + 1) * HD, px * HD:(px + 1) * HD] = w_ref[3 * dy + dx]

    columns = [x] + [(x + X - step) % X for step in (1, 3, 2)]
    staged(0)
    staged(1)
    for column in columns:
        onward(0, column)
    staged(2)
    for column in columns:
        onward(1, column)

    region_len = lens_ref[seq // HEADS]
    key_slot = lax.broadcasted_iota(jnp.int32, (1, n_seq * TOK), 1)
    bias = jnp.where(key_slot < region_len, 0.0, -1e30).astype(F32)
    factor = math.log2(math.e) / math.sqrt(HD)
    for array in range(2):
        wait_bytes(landed[array].at[pl.ds(0, Z - 1)], rz.at[array])

    def powers(index, _):
        query = rq[index].reshape(X * TOK, HD)
        keys = rk[...].reshape(n_seq * TOK, HD)
        scores = lax.dot_general(query, keys, (((1,), (1,)), ((), ())), preferred_element_type=F32) + bias
        top = jnp.max(scores, axis=1, keepdims=True)
        power = jnp.exp2((scores - top) * factor)
        sums[index] = jnp.sum(power, axis=1, keepdims=True)
        probs[index] = power.astype(BF16)
        return 0

    for quarter in range(4):
        lax.fori_loop(2 * quarter, 2 * quarter + 2, powers, 0)
        onward(2, columns[quarter])
    wait_bytes(rv.at[pl.ds(0, Z - 1)], rz.at[2])

    def mixed(step):
        to = (z + step) % Z
        out = jnp.dot(probs[to], rv[...].reshape(n_seq * TOK, HD), preferred_element_type=F32) / sums[to]
        o_mid[to] = out.astype(BF16).reshape(X, TOK, HD)
        return o_mid.at[to]

    for step in far_first:
        block = mixed(step)
        if step == 4:
            remote(block, o_hold, so, rro, z_device(half)).start()
        else:
            remote(block, o_in.at[z], so, ro.at[step - 1], z_device(step)).start()
    own = mixed(0)

    def along_x(blocks, index):
        for step in (2, 1, 3):
            remote(blocks.at[index, (x + step) % X], att.at[index, x], sx2, rx2.at[step - 1], x_device(step)).start()
        att[index, x] = blocks[index, x]

    wait_bytes(o_hold, rro)
    remote(o_hold, o_in.at[(z + Z - half) % Z], so, ro.at[3], z_device(half)).start()
    along_x(o_mid, z)
    for step in (1, 7, 2, 6, 3, 5, 4):
        index = (z + Z - step) % Z
        wait_bytes(o_in.at[index], ro.at[step - 1])
        along_x(o_in, index)
    for step in range(1, X):
        wait_bytes(att.at[pl.ds(0, 2)], rx2.at[step - 1])

    row_of = lax.broadcasted_iota(jnp.int32, (TOK, HD), 0)

    def put_sides(row, region, first, last):
        rows = pl.ds(region * TOK, TOK)
        before = jnp.where(row_of == 0, 0.0, pltpu.roll(last, 1, 0))
        after = jnp.where(row_of == TOK - 1, 0.0, pltpu.roll(first, TOK - 1, 0))
        ext[row, rows, 0:HD] = before.astype(BF16)
        ext[row, rows, 5 * HD:6 * HD] = after.astype(BF16)

    for region in range(2):
        values = att[4 * region:4 * region + 4].astype(F32)
        count = 1.0 / (HEADS * HD)
        mean = jnp.sum(jnp.sum(values, axis=(0, 1)), axis=1, keepdims=True) * count
        centered = values - mean
        var = jnp.sum(jnp.sum(centered * centered, axis=(0, 1)), axis=1, keepdims=True) * count
        scale = lax.rsqrt(var + 1e-05)
        live = seq * TOK + row_of < lens_ref[region]
        for py in range(PATCH):
            line = []
            for px in range(PATCH):
                head = PATCH * py + px
                normed = centered[py, px] * scale * gain_ref[head:head + 1, :]
                normed = jnp.where(live, normed, 0.0)
                ext[py + 1, region * TOK:(region + 1) * TOK, (px + 1) * HD:(px + 2) * HD] = normed.astype(BF16)
                line.append(normed)
            put_sides(py + 1, region, line[0], line[3])

    middle = pl.ds(HD, PATCH * HD)
    down = remote(ext.at[4, :, middle], ext.at[0, :, middle], sh.at[0], rh.at[0], (dp, (seq + 1) % n_seq))
    up = remote(ext.at[1, :, middle], ext.at[5, :, middle], sh.at[1], rh.at[1], (dp, (seq + n_seq - 1) % n_seq))

    @pl.when(seq < n_seq - 1)
    def _():
        down.start()

    @pl.when(seq > 0)
    def _():
        up.start()

    def lines(low, high):
        return ext[low:high].reshape((high - low) * 2 * TOK, 6 * HD)

    def turned(low, high):
        return cot_t[:, low * 2 * TOK:high * 2 * TOK]

    def grad_of(low, high, first):
        return jnp.dot(turned(low, high), lines(first, first + high - low), preferred_element_type=F32)

    grads[1] = grad_of(0, 4, 1)
    grads[0] = grad_of(1, 4, 1)
    grads[2] = grad_of(0, 3, 2)

    @pl.when(seq < n_seq - 1)
    def _():
        down.wait_send()
        wait_bytes(ext.at[5, :, middle], rh.at[1])

    @pl.when(seq > 0)
    def _():
        up.wait_send()
        wait_bytes(ext.at[0, :, middle], rh.at[0])

    @pl.when(seq == 0)
    def _():
        ext[0] = jnp.zeros((2 * TOK, 6 * HD), BF16)

    @pl.when(seq == n_seq - 1)
    def _():
        ext[5] = jnp.zeros((2 * TOK, 6 * HD), BF16)

    for row in (0, 5):
        for region in range(2):
            rows = pl.ds(region * TOK, TOK)
            put_sides(row, region, ext[row, rows, HD:2 * HD].astype(F32), ext[row, rows, 4 * HD:5 * HD].astype(F32))
    grads[0] += grad_of(0, 1, 0)
    grads[2] += grad_of(3, 4, 5)
    for dy in range(3):
        for dx in range(3):
            total = grads[dy, 0:HD, dx * HD:(dx + 1) * HD]
            for px in range(1, PATCH):
                total += grads[dy, px * HD:(px + 1) * HD, (px + dx) * HD:(px + dx + 1) * HD]
            taps[3 * dy + dx] = total.T.reshape(16, 8, HD)

    swap = remote(taps.at[:, pl.ds(8 * (1 - core), 8)], buf1, s1, r1, partner)
    swap.start()
    swap.wait()
    acc1[...] = taps[:, pl.ds(8 * core, 8)] + buf1[...]
    copies = []
    for step in range(1, X):
        to = (x + step) % X
        copy = remote(acc1.at[:, pl.ds(2 * to, 2)], buf2.at[step - 1], s2.at[step - 1], r2.at[step - 1],
                      x_device(step))
        copy.start()
        copies.append(copy)
    for copy in copies:
        copy.wait()
    acc2[...] = (acc1[:, pl.ds(2 * x, 2)] + buf2[0]) + (buf2[1] + buf2[2])
    offset = (member + n_yz - core) % n_yz
    for tile in range(OWNED):
        owner = (3 * tile + core) % n_yz

        @pl.when(owner != member)
        def _():
            remote(acc2.at[tile // 2, tile % 2], buf3.at[member], s3, r3, yz_device(owner)).start()

    decoded = jnp.dot(lines(0, 4), wide[0], preferred_element_type=F32)
    decoded += jnp.dot(lines(1, 5), wide[1], preferred_element_type=F32)
    decoded += jnp.dot(lines(2, 6), wide[2], preferred_element_type=F32)
    for row in range(PATCH):
        for region in range(2):
            low = (row * 2 + region) * TOK
            for px in range(PATCH):
                grid[region, pl.ds(px, TOK, stride=PATCH), :] = decoded[low:low + TOK, px * HD:(px + 1) * HD]
            dec_ref[region, row] = grid[region].astype(BF16)

    mine = offset // 3
    owns = jnp.logical_and(offset % 3 == 0, mine < OWNED)

    @pl.when(owns)
    def _():
        wait_bytes(buf3.at[pl.ds(0, OWNED - 1)], s3)
        wait_bytes(buf3.at[pl.ds(0, n_yz - 1)], r3)
        buf3[member] = acc2[mine // 2, mine % 2]
        fin[mine // 2, mine % 2] = jnp.sum(buf3[...], axis=0) * (1.0 / math.sqrt(PATCH * PATCH * TOK))
        part = fin.at[mine // 2, mine % 2]

        def spread(step, _):
            remote(part, part, s4, r4, yz_device((member + step) % n_yz)).start()
            return 0

        lax.fori_loop(1, n_yz, spread, 0)
        wait_bytes(buf3.at[pl.ds(0, n_yz - 1)], s4)
        wait_bytes(buf3.at[pl.ds(0, OWNED - 1)], r4)

    @pl.when(jnp.logical_not(owns))
    def _():
        wait_bytes(buf3.at[pl.ds(0, OWNED)], s3)
        wait_bytes(buf3.at[pl.ds(0, OWNED)], r4)

    def place(which):
        return wg_ref.at[:, pl.ds(8 * core + 2 * which, 2)]

    copies = []
    for step in range(1, X):
        copy = remote(fin, place(x), s5.at[step - 1], r5.at[step - 1], x_device(step))
        copy.start()
        copies.append(copy)
    wg_ref[:, pl.ds(8 * core + 2 * x, 2)] = fin[...]
    forwards = [remote(fin, place(x), s6.at[0], r6.at[0], partner)]
    forwards[0].start()
    for step in range(1, X):
        copies[step - 1].wait()
        came = place((x + X - step) % X)
        forward = remote(came, came, s6.at[step], r6.at[step], partner)
        forward.start()
        forwards.append(forward)

    for copy in x_copies:
        copy.wait_send()
    for array in range(3):
        wait_bytes(landed[array], sz.at[array])
    wait_bytes(o_in, so)
    wait_bytes(att.at[pl.ds(0, 6)], sx2)
    for forward in forwards:
        forward.wait()


def body(query_rows, key_rows, value_rows, region_lengths, norm_gain, conv_weight, cotangent):
    n_dp = lax.axis_size("dp")
    n_yz = (n_dp // 2) * Z

    def items(rows):
        return rows.reshape(TOK, X * Z, HD).transpose(1, 0, 2).reshape(Z, X, TOK, HD)

    vmem = pl.BlockSpec(memory_space=pltpu.VMEM)
    dma = pltpu.SemaphoreType.DMA
    decoded, grad = pl.pallas_call(
        functools.partial(step_kernel, n_dp),
        out_shape=(jax.ShapeDtypeStruct((2, 4, 256, 128), BF16), jax.ShapeDtypeStruct((9, 16, 8, 128), F32)),
        in_specs=[pl.BlockSpec(memory_space=pltpu.SMEM)] + [vmem] * 6,
        out_specs=(vmem, vmem),
        scratch_shapes=[
            pltpu.VMEM((3, Z, X, TOK, HD), BF16),
            pltpu.VMEM((Z, X, TOK, HD), BF16),
            pltpu.VMEM((Z, X, TOK, HD), BF16),
            pltpu.VMEM((Z, X, TOK, HD), BF16),
            pltpu.VMEM((3, X, TOK, HD), BF16),
            pltpu.VMEM((Z, X * TOK, X * Z * TOK), BF16),
            pltpu.VMEM((Z, X * TOK, 1), F32),
            pltpu.VMEM((Z, X, TOK, HD), BF16),
            pltpu.VMEM((Z, X, TOK, HD), BF16),
            pltpu.VMEM((X, TOK, HD), BF16),
            pltpu.VMEM((Z, X, TOK, HD), BF16),
            pltpu.VMEM((6, 2 * TOK, 6 * HD), BF16),
            pltpu.VMEM((4 * HD, 8 * TOK), BF16),
            pltpu.VMEM((2, PATCH * TOK, HD), F32),
            pltpu.VMEM((3, 6 * HD, 4 * HD), BF16),
            pltpu.VMEM((3, 4 * HD, 6 * HD), F32),
            pltpu.VMEM((9, 16, 8, HD), F32),
            pltpu.VMEM((9, 8, 8, HD), F32),
            pltpu.VMEM((9, 8, 8, HD), F32),
            pltpu.VMEM((3, 9, 2, 8, HD), F32),
            pltpu.VMEM((9, 2, 8, HD), F32),
            pltpu.VMEM((n_yz, 8, HD), F32),
            pltpu.VMEM((9, 2, 8, HD), F32),
            dma((3, 3)), dma((3, 3)), dma((3,)), dma((3,)), dma((3, X)),
            dma, dma((7,)), dma, dma, dma((3,)), dma((2,)), dma((2,)),
            dma, dma, dma((3,)), dma((3,)), dma, dma, dma, dma, dma((3,)), dma((3,)), dma((4,)), dma((4,)),
        ],
        compiler_params=pltpu.CompilerParams(
            collective_id=0, has_side_effects=True, vmem_limit_bytes=60 * 1024 * 1024
        ),
        name="region_step",
    )(
        region_lengths,
        items(query_rows),
        items(key_rows),
        items(value_rows),
        norm_gain.reshape(HEADS, HD),
        conv_weight,
        cotangent,
    )
    return decoded, grad.reshape(9, 128, 128)


def solution(mesh):
    placed = (
        P("seq", "dp", None),
        P("seq", "dp", None),
        P("seq", "dp", None),
        P("dp"),
        P(),
        P(),
        P("dp", "seq", None, None),
    )
    return jax.shard_map(
        body,
        mesh=mesh,
        in_specs=placed,
        out_specs=(P("dp", "seq", None, None), P()),
        check_vma=False,
    )
```

```python
import functools
import math

import jax
import jax.numpy as jnp
from jax import lax
from jax.experimental import pallas as pl
from jax.experimental.pallas import tpu as pltpu
from jax.sharding import PartitionSpec as P

HEADS = 16
PATCH = 4
MESH = pl.DeviceIdType.MESH
X, Z = 4, 8
TOK, HD = 64, 128
OWNED = 18
F32, BF16 = jnp.float32, jnp.bfloat16


def remote(src, dst, send, recv, device):
    return pltpu.make_async_remote_copy(
        src_ref=src, dst_ref=dst, send_sem=send, recv_sem=recv, device_id=device, device_id_type=MESH
    )


def wait_bytes(ref, sem):
    pltpu.make_async_copy(ref, ref, sem).wait()


def step_kernel(n_dp, lens_ref, q_hbm, k_hbm, v_hbm, gain_ref, w_hbm, cot_hbm, dec_ref, wg_ref,
                raw, w_ref, cot_ref, cot_side, pairs, split, stage, rk, rq, rv, hold, probs, sums, o_mid, o_in, o_hold, att, ext, cot_t, grid, wide,
                taps, buf1, acc1, buf2, acc2, buf3, buf4, fin, whole,
                load, sx, rx, sz, rz, rzq, rr, so, ro, rro, sx2, rx2, sh, rh, sc, rc,
                s1, r1, s2, r2, s3, r3, s4, r4, s5, r5, s6, r6):
    dp, seq = lax.axis_index("dp"), lax.axis_index("seq")
    n_seq = X * Z
    n_yz = (n_dp // 2) * Z
    core, z, x = dp % 2, seq // X, seq % X
    member = (dp // 2) * Z + z
    partner = (dp + 1 - 2 * core, seq)
    half = 2 + 4 * core

    def x_device(step):
        return (dp, z * X + (x + step) % X)

    def z_device(step):
        return (dp, ((z + step) % Z) * X + x)

    def yz_device(index):
        return ((index // Z) * 2 + core, (index % Z) * X + x)

    loads = [pltpu.make_async_copy(src, dst, load.at[i]) for i, (src, dst) in enumerate((
        (k_hbm, raw.at[0]), (q_hbm, raw.at[1]), (v_hbm, raw.at[2]), (cot_hbm, cot_ref), (w_hbm, w_ref)))]
    for copy in loads:
        copy.start()

    barrier = pltpu.get_barrier_semaphore()

    def signal(device):
        pl.semaphore_signal(barrier, inc=1, device_id=device, device_id_type=MESH)

    def greet(step, _):
        signal(yz_device((member + step) % n_yz))
        return 0

    for step in range(1, X):
        signal(x_device(step))
    lax.fori_loop(1, n_yz, greet, 0)
    signal(partner)
    signal((dp, (seq + 1) % n_seq))
    signal((dp, (seq + n_seq - 1) % n_seq))

    for array in range(3):
        loads[array].wait()
        for head in range(HEADS):
            both = raw[array, :, :, head * HD:(head + 1) * HD].astype(F32)
            pairs[head % 4] = both.reshape(2 * TOK, HD)
            for region in range(2):
                item = region * HEADS + head
                split[array, item // X, item % X] = pairs[head % 4, pl.ds(region, TOK, stride=2), :].astype(BF16)
    pl.semaphore_wait(barrier, (X - 1) + (n_yz - 1) + 1 + 2)

    landed = (rk, rq, rv)
    far_first = (4, 3, 5, 2, 6, 1, 7)

    x_copies = []
    for array in range(3):
        for step in (1, 3, 2):
            copy = remote(split.at[array, :, (x + step) % X], stage.at[array, :, x],
                          sx.at[array, step - 1], rx.at[array, step - 1], x_device(step))
            copy.start()
            x_copies.append(copy)

    def arrival(array, step):
        return (rz.at[0], rzq.at[step - 1], rz.at[1])[array]

    def along_z(array, blocks, column, step):
        block = blocks.at[(z + step) % Z, column]
        if step == 4:
            remote(block, hold.at[array, column], sz.at[array], rr.at[array, column], z_device(half)).start()
        else:
            remote(block, landed[array].at[z, column], sz.at[array], arrival(array, step), z_device(step)).start()

    others = [(x + X - step) % X for step in (1, 3, 2)]

    def came(array, number):
        wait_bytes(stage.at[array, :, others[number]], rx.at[array, (1, 3, 2)[number] - 1])
        landed[array][z, others[number]] = stage[array, z, others[number]]

    def onward(array, column):
        wait_bytes(hold.at[array, column], rr.at[array, column])
        remote(hold.at[array, column], landed[array].at[(z + Z - half) % Z, column], sz.at[array], arrival(array, 4),
               z_device(half)).start()

    for array in range(3):
        for step in far_first:
            along_z(array, split.at[array], x, step)
        landed[array][z, x] = split[array, z, x]

    loads[3].wait()
    loads[4].wait()

    def turn(row, first, second):
        grid[0], grid[1] = first.astype(F32), second.astype(F32)
        low = (row + 1) * 2 * TOK
        for px in range(PATCH):
            part = [grid[region, pl.ds(px, TOK, stride=PATCH), :] for region in range(2)]
            cot_t[px * HD:(px + 1) * HD, low:low + 2 * TOK] = jnp.concatenate(part).T.astype(BF16)

    for row in range(PATCH):
        turn(row, cot_ref[0, row], cot_ref[1, row])
    wide[...] = jnp.zeros_like(wide)
    for dy in range(3):
        for dx in range(3):
            for px in range(PATCH):
                wide[dy, (px + dx) * HD:(px + dx + 1) * HD, px * HD:(px + 1) * HD] = w_ref[3 * dy + dx]

    columns = [x] + others
    for number in range(3):
        came(0, number)
        for step in far_first:
            along_z(0, stage.at[0], others[number], step)
    for number in range(3):
        came(1, number)
    for step in far_first:
        for column in others:
            along_z(1, stage.at[1], column, step)
    for column in columns:
        onward(0, column)

    region_len = lens_ref[seq // HEADS]
    key_slot = lax.broadcasted_iota(jnp.int32, (1, n_seq * TOK), 1)
    bias = jnp.where(key_slot < region_len, 0.0, -1e30).astype(F32)
    factor = math.log2(math.e) / math.sqrt(HD)

    def powers(step):
        index = (z + Z - step) % Z
        if step:
            wait_bytes(rq.at[index], rzq.at[step - 1])
        query = rq[index].reshape(X * TOK, HD)
        keys = rk[...].reshape(n_seq * TOK, HD)
        scores = lax.dot_general(query, keys, (((1,), (1,)), ((), ())), preferred_element_type=F32) + bias
        top = jnp.max(scores, axis=1, keepdims=True)
        power = jnp.exp2((scores - top) * factor)
        sums[index] = jnp.sum(power, axis=1, keepdims=True)
        probs[index] = power.astype(BF16)

    wait_bytes(rk.at[pl.ds(0, Z - 1)], rz.at[0])
    powers(0)
    for number in range(3):
        came(2, number)
        for step in far_first:
            along_z(2, stage.at[2], others[number], step)
    for column in columns:
        onward(1, column)

    cot_down = remote(cot_ref.at[:, 3], cot_side.at[0], sc.at[0], rc.at[0], (dp, (seq + 1) % n_seq))
    cot_up = remote(cot_ref.at[:, 0], cot_side.at[1], sc.at[1], rc.at[1], (dp, (seq + n_seq - 1) % n_seq))

    @pl.when(x < X - 1)
    def _():
        cot_down.start()

    @pl.when(x > 0)
    def _():
        cot_up.start()

    powers(3)
    powers(5)
    powers(2)
    for column, step in zip(columns, (6, 1, 7)):
        powers(step)
        onward(2, column)
    onward(2, columns[3])
    powers(4)
    wait_bytes(rv.at[pl.ds(0, Z - 1)], rz.at[1])

    def mixed(step):
        to = (z + step) % Z
        out = jnp.dot(probs[to], rv[...].reshape(n_seq * TOK, HD), preferred_element_type=F32) / sums[to]
        o_mid[to] = out.astype(BF16).reshape(X, TOK, HD)

    def home(blocks, column, step):
        block = blocks.at[(z + step) % Z, column]
        if step == 4:
            remote(block, o_hold.at[column], so, rro.at[column], z_device(half)).start()
        else:
            remote(block, att.at[z, column], so, ro, z_device(step)).start()

    for step in far_first + (0,):
        mixed(step)
        to = (z + step) % Z
        for side in (2, 1, 3):
            block = o_mid.at[to, (x + side) % X]
            if step:
                remote(block, o_in.at[to, x], sx2, rx2.at[step - 1, side - 1], x_device(side)).start()
            else:
                remote(block, att.at[z, x], sx2, rx2.at[7, side - 1], x_device(side)).start()
        if step:
            home(o_mid, x, step)
    att[z, x] = o_mid[z, x]

    @pl.when(jnp.logical_and(x == X - 1, seq < n_seq - 1))
    def _():
        cot_down.start()

    @pl.when(jnp.logical_and(x == 0, seq > 0))
    def _():
        cot_up.start()

    def passing(step):
        for side in (1, 3, 2):
            column = (x + X - side) % X
            wait_bytes(o_in.at[(z + step) % Z, column], rx2.at[step - 1, side - 1])
            home(o_in, column, step)

    for step in (4, 3, 5, 2, 6):
        passing(step)
    for column in columns:
        wait_bytes(o_hold.at[column], rro.at[column])
        remote(o_hold.at[column], att.at[(z + Z - half) % Z, column], so, ro, z_device(half)).start()
    for step in (1, 7):
        passing(step)
    for side in range(1, X):
        wait_bytes(att.at[z, (x + X - side) % X], rx2.at[7, side - 1])
    wait_bytes(att.at[pl.ds(0, Z - 1)], ro)

    row_of = lax.broadcasted_iota(jnp.int32, (TOK, HD), 0)

    def put_sides(row, region, first, last):
        rows = pl.ds(region * TOK, TOK)
        before = jnp.where(row_of == 0, 0.0, pltpu.roll(last, 1, 0))
        after = jnp.where(row_of == TOK - 1, 0.0, pltpu.roll(first, TOK - 1, 0))
        ext[row, rows, 0:HD] = before.astype(BF16)
        ext[row, rows, 5 * HD:6 * HD] = after.astype(BF16)

    for region in range(2):
        values = att[4 * region:4 * region + 4].astype(F32)
        count = 1.0 / (HEADS * HD)
        mean = jnp.sum(jnp.sum(values, axis=(0, 1)), axis=1, keepdims=True) * count
        centered = values - mean
        var = jnp.sum(jnp.sum(centered * centered, axis=(0, 1)), axis=1, keepdims=True) * count
        scale = lax.rsqrt(var + 1e-05)
        live = seq * TOK + row_of < lens_ref[region]
        for py in range(PATCH):
            line = []
            for px in range(PATCH):
                head = PATCH * py + px
                normed = centered[py, px] * scale * gain_ref[head:head + 1, :]
                normed = jnp.where(live, normed, 0.0)
                ext[py + 1, region * TOK:(region + 1) * TOK, (px + 1) * HD:(px + 2) * HD] = normed.astype(BF16)
                line.append(normed)
            put_sides(py + 1, region, line[0], line[3])

    middle = pl.ds(HD, PATCH * HD)
    down = remote(ext.at[4, :, middle], ext.at[0, :, middle], sh.at[0], rh.at[0], (dp, (seq + 1) % n_seq))
    up = remote(ext.at[1, :, middle], ext.at[5, :, middle], sh.at[1], rh.at[1], (dp, (seq + n_seq - 1) % n_seq))

    @pl.when(seq < n_seq - 1)
    def _():
        down.start()

    @pl.when(seq > 0)
    def _():
        up.start()

    def lines(low, high):
        return ext[low:high].reshape((high - low) * 2 * TOK, 6 * HD)

    def taps_of(dy):
        low = (2 - dy) * 2 * TOK
        block = jnp.dot(cot_t[:, low:low + PATCH * 2 * TOK], lines(1, 5), preferred_element_type=F32)
        for dx in range(3):
            total = block[0:HD, dx * HD:(dx + 1) * HD]
            for px in range(1, PATCH):
                total += block[px * HD:(px + 1) * HD, (px + dx) * HD:(px + dx + 1) * HD]
            taps[3 * dy + dx] = total.T.reshape(16, 8, HD)

    def three(ref, dy, *rest):
        return ref.at[(pl.ds(3 * dy, 3),) + rest]

    def to_core(dy):
        return remote(three(taps, dy, pl.ds(8 * (1 - core), 8)), three(buf1, dy), s1.at[dy], r1.at[dy], partner)

    def to_x(dy, step):
        return remote(three(acc1, dy, pl.ds(2 * ((x + step) % X), 2)), buf2.at[step - 1, pl.ds(3 * dy, 3)],
                      s2.at[dy, step - 1], r2.at[dy, step - 1], x_device(step))

    def cores_done(dy):
        to_core(dy).wait()
        some = slice(3 * dy, 3 * dy + 3)
        acc1[some] = taps[some, pl.ds(8 * core, 8)] + buf1[some]
        for step in (2, 1, 3):
            to_x(dy, step).start()

    taps_of(1)
    to_core(1).start()

    @pl.when(seq < n_seq - 1)
    def _():
        cot_down.wait_send()
        wait_bytes(cot_side.at[1], rc.at[1])

    @pl.when(seq > 0)
    def _():
        cot_up.wait_send()
        wait_bytes(cot_side.at[0], rc.at[0])

    @pl.when(seq == 0)
    def _():
        cot_side[0] = jnp.zeros((2, PATCH * TOK, HD), BF16)

    @pl.when(seq == n_seq - 1)
    def _():
        cot_side[1] = jnp.zeros((2, PATCH * TOK, HD), BF16)

    turn(PATCH, cot_side[1, 0], cot_side[1, 1])
    taps_of(0)
    to_core(0).start()
    cores_done(1)
    turn(-1, cot_side[0, 0], cot_side[0, 1])
    taps_of(2)
    to_core(2).start()
    cores_done(0)
    cores_done(2)
    for dy in (1, 0, 2):
        for step in range(1, X):
            to_x(dy, step).wait()
        some = slice(3 * dy, 3 * dy + 3)
        acc2[some] = (acc1[some, pl.ds(2 * x, 2)] + buf2[0, some]) + (buf2[1, some] + buf2[2, some])
        for tile in range(6 * dy, 6 * dy + 6):
            owner = (3 * tile + core) % n_yz

            @pl.when(owner != member)
            def _():
                remote(acc2.at[tile // 2, tile % 2], buf3.at[member], s3, r3, yz_device(owner)).start()
    offset = (member + n_yz - core) % n_yz

    @pl.when(seq < n_seq - 1)
    def _():
        down.wait_send()
        wait_bytes(ext.at[5, :, middle], rh.at[1])

    @pl.when(seq > 0)
    def _():
        up.wait_send()
        wait_bytes(ext.at[0, :, middle], rh.at[0])

    @pl.when(seq == 0)
    def _():
        ext[0] = jnp.zeros((2 * TOK, 6 * HD), BF16)

    @pl.when(seq == n_seq - 1)
    def _():
        ext[5] = jnp.zeros((2 * TOK, 6 * HD), BF16)

    for row in (0, 5):
        for region in range(2):
            rows = pl.ds(region * TOK, TOK)
            put_sides(row, region, ext[row, rows, HD:2 * HD].astype(F32), ext[row, rows, 4 * HD:5 * HD].astype(F32))

    decoded = jnp.dot(lines(0, 4), wide[0], preferred_element_type=F32)
    decoded += jnp.dot(lines(1, 5), wide[1], preferred_element_type=F32)
    decoded += jnp.dot(lines(2, 6), wide[2], preferred_element_type=F32)
    for row in range(PATCH):
        for region in range(2):
            low = (row * 2 + region) * TOK
            for px in range(PATCH):
                grid[region, pl.ds(px, TOK, stride=PATCH), :] = decoded[low:low + TOK, px * HD:(px + 1) * HD]
            dec_ref[region, row] = grid[region].astype(BF16)

    mine = offset // 3
    owns = jnp.logical_and(offset % 3 == 0, mine < OWNED)

    @pl.when(owns)
    def _():
        wait_bytes(buf3.at[pl.ds(0, OWNED - 1)], s3)
        wait_bytes(buf3.at[pl.ds(0, n_yz - 1)], r3)
        buf3[member] = acc2[mine // 2, mine % 2]
        total = jnp.sum(buf3[...], axis=0) * (1.0 / math.sqrt(PATCH * PATCH * TOK))
        fin[mine // 2, mine % 2] = total.astype(BF16)
        part = fin.at[mine // 2, mine % 2]

        def spread(step, _):
            remote(part, part, s4, r4, yz_device((member + step) % n_yz)).start()
            return 0

        lax.fori_loop(1, n_yz, spread, 0)
        wait_bytes(buf4.at[pl.ds(0, n_yz - 1)], s4)
        wait_bytes(buf4.at[pl.ds(0, OWNED - 1)], r4)

    @pl.when(jnp.logical_not(owns))
    def _():
        wait_bytes(buf3.at[pl.ds(0, OWNED)], s3)
        wait_bytes(buf4.at[pl.ds(0, OWNED)], r4)

    def place(which):
        return whole.at[:, pl.ds(8 * core + 2 * which, 2)]

    copies = []
    for step in range(1, X):
        copy = remote(fin, place(x), s5.at[step - 1], r5.at[step - 1], x_device(step))
        copy.start()
        copies.append(copy)
    whole[:, pl.ds(8 * core + 2 * x, 2)] = fin[...]
    forwards = [remote(fin, place(x), s6.at[0], r6.at[0], partner)]
    forwards[0].start()
    for step in range(1, X):
        copies[step - 1].wait()
        block = place((x + X - step) % X)
        forward = remote(block, block, s6.at[step], r6.at[step], partner)
        forward.start()
        forwards.append(forward)

    for copy in x_copies:
        copy.wait_send()
    for array in range(3):
        wait_bytes(landed[array], sz.at[array])
    wait_bytes(o_in, so)
    wait_bytes(att.at[pl.ds(0, 6)], sx2)
    for forward in forwards:
        forward.wait()
    wg_ref[...] = whole[...].astype(F32)


def body(query_rows, key_rows, value_rows, region_lengths, norm_gain, conv_weight, cotangent):
    n_dp = lax.axis_size("dp")
    n_yz = (n_dp // 2) * Z
    hbm = pl.BlockSpec(memory_space=pl.ANY)
    vmem = pl.BlockSpec(memory_space=pltpu.VMEM)
    dma = pltpu.SemaphoreType.DMA
    decoded, grad = pl.pallas_call(
        functools.partial(step_kernel, n_dp),
        out_shape=(jax.ShapeDtypeStruct((2, 4, 256, 128), BF16), jax.ShapeDtypeStruct((9, 16, 8, 128), F32)),
        in_specs=[pl.BlockSpec(memory_space=pltpu.SMEM), hbm, hbm, hbm, vmem, hbm, hbm],
        out_specs=(vmem, vmem),
        scratch_shapes=[
            pltpu.VMEM((3, TOK, 2, HEADS * HD), BF16),
            pltpu.VMEM((9, HD, HD), BF16),
            pltpu.VMEM((2, PATCH, PATCH * TOK, HD), BF16),
            pltpu.VMEM((2, 2, PATCH * TOK, HD), BF16),
            pltpu.VMEM((4, 2 * TOK, HD), F32),
            pltpu.VMEM((3, Z, X, TOK, HD), BF16),
            pltpu.VMEM((3, Z, X, TOK, HD), BF16),
            pltpu.VMEM((Z, X, TOK, HD), BF16),
            pltpu.VMEM((Z, X, TOK, HD), BF16),
            pltpu.VMEM((Z, X, TOK, HD), BF16),
            pltpu.VMEM((3, X, TOK, HD), BF16),
            pltpu.VMEM((Z, X * TOK, X * Z * TOK), BF16),
            pltpu.VMEM((Z, X * TOK, 1), F32),
            pltpu.VMEM((Z, X, TOK, HD), BF16),
            pltpu.VMEM((Z, X, TOK, HD), BF16),
            pltpu.VMEM((X, TOK, HD), BF16),
            pltpu.VMEM((Z, X, TOK, HD), BF16),
            pltpu.VMEM((6, 2 * TOK, 6 * HD), BF16),
            pltpu.VMEM((4 * HD, 6 * 2 * TOK), BF16),
            pltpu.VMEM((2, PATCH * TOK, HD), F32),
            pltpu.VMEM((3, 6 * HD, 4 * HD), BF16),
            pltpu.VMEM((9, 16, 8, HD), F32),
            pltpu.VMEM((9, 8, 8, HD), F32),
            pltpu.VMEM((9, 8, 8, HD), F32),
            pltpu.VMEM((3, 9, 2, 8, HD), F32),
            pltpu.VMEM((9, 2, 8, HD), F32),
            pltpu.VMEM((n_yz, 8, HD), F32),
            pltpu.VMEM((n_yz, 8, HD), BF16),
            pltpu.VMEM((9, 2, 8, HD), BF16),
            pltpu.VMEM((9, 16, 8, HD), BF16),
            dma((5,)), dma((3, 3)), dma((3, 3)), dma((3,)), dma((2,)), dma((7,)), dma((3, X)),
            dma, dma, dma((X,)), dma, dma((8, 3)), dma((2,)), dma((2,)), dma((2,)), dma((2,)),
            dma((3,)), dma((3,)), dma((3, 3)), dma((3, 3)), dma, dma, dma, dma, dma((3,)), dma((3,)), dma((4,)), dma((4,)),
        ],
        compiler_params=pltpu.CompilerParams(
            collective_id=0, has_side_effects=True, vmem_limit_bytes=60 * 1024 * 1024
        ),
        name="region_step",
    )(
        region_lengths,
        query_rows,
        key_rows,
        value_rows,
        norm_gain.reshape(HEADS, HD),
        conv_weight,
        cotangent,
    )
    return decoded, grad.reshape(9, 128, 128)


def solution(mesh):
    placed = (
        P("seq", "dp", None),
        P("seq", "dp", None),
        P("seq", "dp", None),
        P("dp"),
        P(),
        P(),
        P("dp", "seq", None, None),
    )
    return jax.shard_map(
        body,
        mesh=mesh,
        in_specs=placed,
        out_specs=(P("dp", "seq", None, None), P()),
        check_vma=False,
    )
```

```python
import functools
import math

import jax
import jax.numpy as jnp
from jax import lax
from jax.experimental import pallas as pl
from jax.experimental.pallas import tpu as pltpu
from jax.sharding import PartitionSpec as P

HEADS = 16
PATCH = 4
MESH = pl.DeviceIdType.MESH
X, Z = 4, 8
TOK, HD = 64, 128
OWNED = 18
F32, BF16 = jnp.float32, jnp.bfloat16


def remote(src, dst, send, recv, device):
    return pltpu.make_async_remote_copy(
        src_ref=src, dst_ref=dst, send_sem=send, recv_sem=recv, device_id=device, device_id_type=MESH
    )


def wait_bytes(ref, sem):
    pltpu.make_async_copy(ref, ref, sem).wait()


def step_kernel(n_dp, lens_ref, q_hbm, k_hbm, v_hbm, gain_ref, w_hbm, cot_hbm, dec_ref, wg_ref,
                raw, w_ref, cot_ref, cot_side, pairs, split, stage, rk, rq, rv, hold, probs, sums, o_mid, o_in, o_hold, att, ext, cot_t, grid, wide,
                taps, buf1, acc1, buf2, acc2, buf3, buf4, fin, whole,
                inside, load, sx, rx, sz, rz, rzq, rr, so, ro, rro, sx2, rx2, sh, rh, sc, rc,
                s1, r1, s2, r2, s3, r3, s4, r4, s5, r5, s6, r6):
    dp, seq = lax.axis_index("dp"), lax.axis_index("seq")
    n_seq = X * Z
    n_yz = (n_dp // 2) * Z
    core, z, x = dp % 2, seq // X, seq % X
    member = (dp // 2) * Z + z
    partner = (dp + 1 - 2 * core, seq)
    half = 2 + 4 * core

    def x_device(step):
        return (dp, z * X + (x + step) % X)

    def z_device(step):
        return (dp, ((z + step) % Z) * X + x)

    def yz_device(index):
        return ((index // Z) * 2 + core, (index % Z) * X + x)

    loads = [pltpu.make_async_copy(src, dst, load.at[i]) for i, (src, dst) in enumerate((
        (k_hbm, raw.at[0]), (q_hbm, raw.at[1]), (v_hbm, raw.at[2]), (cot_hbm, cot_ref), (w_hbm, w_ref)))]
    for copy in loads:
        copy.start()

    barrier = pltpu.get_barrier_semaphore()

    def signal(device):
        pl.semaphore_signal(barrier, inc=1, device_id=device, device_id_type=MESH)

    n_y = n_dp // 2

    def y_device(step):
        return (((dp // 2 + step) % n_y) * 2 + core, seq)

    for step in range(1, n_y):
        signal(y_device(step))
    for step in range(1, Z):
        signal(z_device(step))
    for step in range(1, X):
        signal(x_device(step))
    signal(partner)
    signal((dp, (seq + 1) % n_seq))
    signal((dp, (seq + n_seq - 1) % n_seq))

    def divide(array):
        loads[array].wait()
        for head in range(HEADS):
            both = raw[array, :, :, head * HD:(head + 1) * HD].astype(F32)
            pairs[head % 4] = both.reshape(2 * TOK, HD)
            for region in range(2):
                item = region * HEADS + head
                split[array, item // X, item % X] = pairs[head % 4, pl.ds(region, TOK, stride=2), :].astype(BF16)

    divide(0)
    pl.semaphore_wait(barrier, (n_y - 1) + (Z - 1) + (X - 1) + 1 + 2)

    landed = (rk, rq, rv)
    far_first = (4, 3, 5, 2, 6, 1, 7)

    x_copies = []

    def along_x(array):
        for step in (1, 3, 2):
            copy = remote(split.at[array, :, (x + step) % X], stage.at[array, :, x],
                          sx.at[array, step - 1], rx.at[array, step - 1], x_device(step))
            copy.start()
            x_copies.append(copy)

    def arrival(array, step):
        return (rz.at[0], rzq.at[step - 1], rz.at[1])[array]

    def along_z(array, blocks, column, step):
        block = blocks.at[(z + step) % Z, column]
        if step == 4:
            remote(block, hold.at[array, column], sz.at[array], rr.at[array, column], z_device(half)).start()
        else:
            remote(block, landed[array].at[z, column], sz.at[array], arrival(array, step), z_device(step)).start()

    others = [(x + X - step) % X for step in (1, 3, 2)]

    def came(array, number):
        wait_bytes(stage.at[array, :, others[number]], rx.at[array, (1, 3, 2)[number] - 1])
        landed[array][z, others[number]] = stage[array, z, others[number]]

    def onward(array, column):
        wait_bytes(hold.at[array, column], rr.at[array, column])
        remote(hold.at[array, column], landed[array].at[(z + Z - half) % Z, column], sz.at[array], arrival(array, 4),
               z_device(half)).start()

    for array in range(3):
        if array:
            divide(array)
        along_x(array)
        for step in far_first:
            along_z(array, split.at[array], x, step)
        landed[array][z, x] = split[array, z, x]

    for step in range(1, n_y):
        pl.semaphore_signal(inside, inc=1, device_id=y_device(step), device_id_type=MESH)

    loads[3].wait()
    loads[4].wait()

    def turn(row, first, second):
        grid[0], grid[1] = first.astype(F32), second.astype(F32)
        low = (row + 1) * 2 * TOK
        for px in range(PATCH):
            part = [grid[region, pl.ds(px, TOK, stride=PATCH), :] for region in range(2)]
            cot_t[px * HD:(px + 1) * HD, low:low + 2 * TOK] = jnp.concatenate(part).T.astype(BF16)

    for row in range(PATCH):
        turn(row, cot_ref[0, row], cot_ref[1, row])
    wide[...] = jnp.zeros_like(wide)
    for dy in range(3):
        for dx in range(3):
            for px in range(PATCH):
                wide[dy, (px + dx) * HD:(px + dx + 1) * HD, px * HD:(px + 1) * HD] = w_ref[3 * dy + dx]

    columns = [x] + others
    for number in range(3):
        came(0, number)
        for step in far_first:
            along_z(0, stage.at[0], others[number], step)
    for number in range(3):
        came(1, number)
    for step in far_first:
        for column in others:
            along_z(1, stage.at[1], column, step)
    for column in columns:
        onward(0, column)

    region_len = lens_ref[seq // HEADS]
    key_slot = lax.broadcasted_iota(jnp.int32, (1, n_seq * TOK), 1)
    bias = jnp.where(key_slot < region_len, 0.0, -1e30).astype(F32)
    factor = math.log2(math.e) / math.sqrt(HD)

    def powers(step):
        index = (z + Z - step) % Z
        if step:
            wait_bytes(rq.at[index], rzq.at[step - 1])
        query = rq[index].reshape(X * TOK, HD)
        keys = rk[...].reshape(n_seq * TOK, HD)
        scores = lax.dot_general(query, keys, (((1,), (1,)), ((), ())), preferred_element_type=F32) + bias
        top = jnp.max(scores, axis=1, keepdims=True)
        power = jnp.exp2((scores - top) * factor)
        sums[index] = jnp.sum(power, axis=1, keepdims=True)
        probs[index] = power.astype(BF16)

    wait_bytes(rk.at[pl.ds(0, Z - 1)], rz.at[0])
    powers(0)
    for number in range(3):
        came(2, number)
        for step in far_first:
            along_z(2, stage.at[2], others[number], step)
    for column in columns:
        onward(1, column)

    cot_down = remote(cot_ref.at[:, 3], cot_side.at[0], sc.at[0], rc.at[0], (dp, (seq + 1) % n_seq))
    cot_up = remote(cot_ref.at[:, 0], cot_side.at[1], sc.at[1], rc.at[1], (dp, (seq + n_seq - 1) % n_seq))

    @pl.when(x < X - 1)
    def _():
        cot_down.start()

    @pl.when(x > 0)
    def _():
        cot_up.start()

    powers(3)
    powers(5)
    powers(2)
    for column, step in zip(columns, (6, 1, 7)):
        powers(step)
        onward(2, column)
    onward(2, columns[3])
    powers(4)
    wait_bytes(rv.at[pl.ds(0, Z - 1)], rz.at[1])

    def mixed(step):
        to = (z + step) % Z
        out = jnp.dot(probs[to], rv[...].reshape(n_seq * TOK, HD), preferred_element_type=F32) / sums[to]
        o_mid[to] = out.astype(BF16).reshape(X, TOK, HD)

    def home(blocks, column, step):
        block = blocks.at[(z + step) % Z, column]
        if step == 4:
            remote(block, o_hold.at[column], so, rro.at[column], z_device(half)).start()
        else:
            remote(block, att.at[z, column], so, ro, z_device(step)).start()

    for step in far_first + (0,):
        mixed(step)
        to = (z + step) % Z
        for side in (2, 1, 3):
            block = o_mid.at[to, (x + side) % X]
            if step:
                remote(block, o_in.at[to, x], sx2, rx2.at[step - 1, side - 1], x_device(side)).start()
            else:
                remote(block, att.at[z, x], sx2, rx2.at[7, side - 1], x_device(side)).start()
        if step:
            home(o_mid, x, step)
    att[z, x] = o_mid[z, x]

    @pl.when(jnp.logical_and(x == X - 1, seq < n_seq - 1))
    def _():
        cot_down.start()

    @pl.when(jnp.logical_and(x == 0, seq > 0))
    def _():
        cot_up.start()

    def passing(step):
        for side in (1, 3, 2):
            column = (x + X - side) % X
            wait_bytes(o_in.at[(z + step) % Z, column], rx2.at[step - 1, side - 1])
            home(o_in, column, step)

    for step in (4, 3, 5, 2, 6):
        passing(step)
    for column in columns:
        wait_bytes(o_hold.at[column], rro.at[column])
        remote(o_hold.at[column], att.at[(z + Z - half) % Z, column], so, ro, z_device(half)).start()
    for step in (1, 7):
        passing(step)
    @pl.when(seq < n_seq - 1)
    def _():
        cot_down.wait_send()
        wait_bytes(cot_side.at[1], rc.at[1])

    @pl.when(seq > 0)
    def _():
        cot_up.wait_send()
        wait_bytes(cot_side.at[0], rc.at[0])

    @pl.when(seq == 0)
    def _():
        cot_side[0] = jnp.zeros((2, PATCH * TOK, HD), BF16)

    @pl.when(seq == n_seq - 1)
    def _():
        cot_side[1] = jnp.zeros((2, PATCH * TOK, HD), BF16)

    turn(PATCH, cot_side[1, 0], cot_side[1, 1])
    turn(-1, cot_side[0, 0], cot_side[0, 1])
    for side in range(1, X):
        wait_bytes(att.at[z, (x + X - side) % X], rx2.at[7, side - 1])
    wait_bytes(att.at[pl.ds(0, Z - 1)], ro)

    row_of = lax.broadcasted_iota(jnp.int32, (TOK, HD), 0)

    def put_sides(row, region, first, last):
        rows = pl.ds(region * TOK, TOK)
        before = jnp.where(row_of == 0, 0.0, pltpu.roll(last, 1, 0))
        after = jnp.where(row_of == TOK - 1, 0.0, pltpu.roll(first, TOK - 1, 0))
        ext[row, rows, 0:HD] = before.astype(BF16)
        ext[row, rows, 5 * HD:6 * HD] = after.astype(BF16)

    for region in range(2):
        values = att[4 * region:4 * region + 4].astype(F32)
        count = 1.0 / (HEADS * HD)
        mean = jnp.sum(jnp.sum(values, axis=(0, 1)), axis=1, keepdims=True) * count
        centered = values - mean
        var = jnp.sum(jnp.sum(centered * centered, axis=(0, 1)), axis=1, keepdims=True) * count
        scale = lax.rsqrt(var + 1e-05)
        live = seq * TOK + row_of < lens_ref[region]
        for py in range(PATCH):
            line = []
            for px in range(PATCH):
                head = PATCH * py + px
                normed = centered[py, px] * scale * gain_ref[head:head + 1, :]
                normed = jnp.where(live, normed, 0.0)
                ext[py + 1, region * TOK:(region + 1) * TOK, (px + 1) * HD:(px + 2) * HD] = normed.astype(BF16)
                line.append(normed)
            put_sides(py + 1, region, line[0], line[3])

    middle = pl.ds(HD, PATCH * HD)
    down = remote(ext.at[4, :, middle], ext.at[0, :, middle], sh.at[0], rh.at[0], (dp, (seq + 1) % n_seq))
    up = remote(ext.at[1, :, middle], ext.at[5, :, middle], sh.at[1], rh.at[1], (dp, (seq + n_seq - 1) % n_seq))

    def lines(low, high):
        return ext[low:high].reshape((high - low) * 2 * TOK, 6 * HD)

    def taps_of(dy):
        low = (2 - dy) * 2 * TOK
        block = jnp.dot(cot_t[:, low:low + PATCH * 2 * TOK], lines(1, 5), preferred_element_type=F32)
        for dx in range(3):
            total = block[0:HD, dx * HD:(dx + 1) * HD]
            for px in range(1, PATCH):
                total += block[px * HD:(px + 1) * HD, (px + dx) * HD:(px + dx + 1) * HD]
            taps[3 * dy + dx] = total.T.reshape(16, 8, HD)

    def three(ref, dy, *rest):
        return ref.at[(pl.ds(3 * dy, 3),) + rest]

    def to_core(dy):
        return remote(three(taps, dy, pl.ds(8 * (1 - core), 8)), three(buf1, dy), s1.at[dy], r1.at[dy], partner)

    def to_x(dy, step):
        return remote(three(acc1, dy, pl.ds(2 * ((x + step) % X), 2)), buf2.at[step - 1, pl.ds(3 * dy, 3)],
                      s2.at[dy, step - 1], r2.at[dy, step - 1], x_device(step))

    def cores_done(dy):
        to_core(dy).wait()
        some = slice(3 * dy, 3 * dy + 3)
        acc1[some] = taps[some, pl.ds(8 * core, 8)] + buf1[some]
        for step in (2, 1, 3):
            to_x(dy, step).start()

    taps_of(1)
    to_core(1).start()

    taps_of(0)
    to_core(0).start()
    cores_done(1)
    taps_of(2)
    to_core(2).start()
    cores_done(0)
    cores_done(2)

    @pl.when(seq < n_seq - 1)
    def _():
        down.start()

    @pl.when(seq > 0)
    def _():
        up.start()

    pl.semaphore_wait(inside, n_y - 1)
    for dy in (1, 0, 2):
        for step in range(1, X):
            to_x(dy, step).wait()
        some = slice(3 * dy, 3 * dy + 3)
        acc2[some] = (acc1[some, pl.ds(2 * x, 2)] + buf2[0, some]) + (buf2[1, some] + buf2[2, some])
        for tile in range(6 * dy, 6 * dy + 6):
            owner = (3 * tile + core) % n_yz

            @pl.when(owner != member)
            def _():
                remote(acc2.at[tile // 2, tile % 2], buf3.at[member], s3, r3, yz_device(owner)).start()
    offset = (member + n_yz - core) % n_yz

    @pl.when(seq < n_seq - 1)
    def _():
        down.wait_send()
        wait_bytes(ext.at[5, :, middle], rh.at[1])

    @pl.when(seq > 0)
    def _():
        up.wait_send()
        wait_bytes(ext.at[0, :, middle], rh.at[0])

    @pl.when(seq == 0)
    def _():
        ext[0] = jnp.zeros((2 * TOK, 6 * HD), BF16)

    @pl.when(seq == n_seq - 1)
    def _():
        ext[5] = jnp.zeros((2 * TOK, 6 * HD), BF16)

    for row in (0, 5):
        for region in range(2):
            rows = pl.ds(region * TOK, TOK)
            put_sides(row, region, ext[row, rows, HD:2 * HD].astype(F32), ext[row, rows, 4 * HD:5 * HD].astype(F32))

    decoded = jnp.dot(lines(0, 4), wide[0], preferred_element_type=F32)
    decoded += jnp.dot(lines(1, 5), wide[1], preferred_element_type=F32)
    decoded += jnp.dot(lines(2, 6), wide[2], preferred_element_type=F32)
    for row in range(PATCH):
        for region in range(2):
            low = (row * 2 + region) * TOK
            for px in range(PATCH):
                grid[region, pl.ds(px, TOK, stride=PATCH), :] = decoded[low:low + TOK, px * HD:(px + 1) * HD]
            dec_ref[region, row] = grid[region].astype(BF16)

    mine = offset // 3
    owns = jnp.logical_and(offset % 3 == 0, mine < OWNED)

    @pl.when(owns)
    def _():
        wait_bytes(buf3.at[pl.ds(0, OWNED - 1)], s3)
        wait_bytes(buf3.at[pl.ds(0, n_yz - 1)], r3)
        buf3[member] = acc2[mine // 2, mine % 2]
        total = jnp.sum(buf3[...], axis=0) * (1.0 / math.sqrt(PATCH * PATCH * TOK))
        fin[mine // 2, mine % 2] = total.astype(BF16)
        part = fin.at[mine // 2, mine % 2]

        def spread(step, _):
            remote(part, part, s4, r4, yz_device((member + step) % n_yz)).start()
            return 0

        lax.fori_loop(1, n_yz, spread, 0)
        wait_bytes(buf4.at[pl.ds(0, n_yz - 1)], s4)
        wait_bytes(buf4.at[pl.ds(0, OWNED - 1)], r4)

    @pl.when(jnp.logical_not(owns))
    def _():
        wait_bytes(buf3.at[pl.ds(0, OWNED)], s3)
        wait_bytes(buf4.at[pl.ds(0, OWNED)], r4)

    def place(which):
        return whole.at[:, pl.ds(8 * core + 2 * which, 2)]

    copies = []
    for step in range(1, X):
        copy = remote(fin, place(x), s5.at[step - 1], r5.at[step - 1], x_device(step))
        copy.start()
        copies.append(copy)
    whole[:, pl.ds(8 * core + 2 * x, 2)] = fin[...]
    forwards = [remote(fin, place(x), s6.at[0], r6.at[0], partner)]
    forwards[0].start()
    for step in range(1, X):
        copies[step - 1].wait()
        block = place((x + X - step) % X)
        forward = remote(block, block, s6.at[step], r6.at[step], partner)
        forward.start()
        forwards.append(forward)

    for copy in x_copies:
        copy.wait_send()
    for array in range(3):
        wait_bytes(landed[array], sz.at[array])
    wait_bytes(o_in, so)
    wait_bytes(att.at[pl.ds(0, 6)], sx2)
    for forward in forwards:
        forward.wait()
    wg_ref[...] = whole[...].astype(F32)


def body(query_rows, key_rows, value_rows, region_lengths, norm_gain, conv_weight, cotangent):
    n_dp = lax.axis_size("dp")
    n_yz = (n_dp // 2) * Z
    hbm = pl.BlockSpec(memory_space=pl.ANY)
    vmem = pl.BlockSpec(memory_space=pltpu.VMEM)
    dma = pltpu.SemaphoreType.DMA
    decoded, grad = pl.pallas_call(
        functools.partial(step_kernel, n_dp),
        out_shape=(pltpu.VMEM((2, 4, 256, 128), BF16), pltpu.VMEM((9, 16, 8, 128), F32)),
        in_specs=[pl.BlockSpec(memory_space=pltpu.SMEM), hbm, hbm, hbm, vmem, hbm, hbm],
        out_specs=(vmem, vmem),
        scratch_shapes=[
            pltpu.VMEM((3, TOK, 2, HEADS * HD), BF16),
            pltpu.VMEM((9, HD, HD), BF16),
            pltpu.VMEM((2, PATCH, PATCH * TOK, HD), BF16),
            pltpu.VMEM((2, 2, PATCH * TOK, HD), BF16),
            pltpu.VMEM((4, 2 * TOK, HD), F32),
            pltpu.VMEM((3, Z, X, TOK, HD), BF16),
            pltpu.VMEM((3, Z, X, TOK, HD), BF16),
            pltpu.VMEM((Z, X, TOK, HD), BF16),
            pltpu.VMEM((Z, X, TOK, HD), BF16),
            pltpu.VMEM((Z, X, TOK, HD), BF16),
            pltpu.VMEM((3, X, TOK, HD), BF16),
            pltpu.VMEM((Z, X * TOK, X * Z * TOK), BF16),
            pltpu.VMEM((Z, X * TOK, 1), F32),
            pltpu.VMEM((Z, X, TOK, HD), BF16),
            pltpu.VMEM((Z, X, TOK, HD), BF16),
            pltpu.VMEM((X, TOK, HD), BF16),
            pltpu.VMEM((Z, X, TOK, HD), BF16),
            pltpu.VMEM((6, 2 * TOK, 6 * HD), BF16),
            pltpu.VMEM((4 * HD, 6 * 2 * TOK), BF16),
            pltpu.VMEM((2, PATCH * TOK, HD), F32),
            pltpu.VMEM((3, 6 * HD, 4 * HD), BF16),
            pltpu.VMEM((9, 16, 8, HD), F32),
            pltpu.VMEM((9, 8, 8, HD), F32),
            pltpu.VMEM((9, 8, 8, HD), F32),
            pltpu.VMEM((3, 9, 2, 8, HD), F32),
            pltpu.VMEM((9, 2, 8, HD), F32),
            pltpu.VMEM((n_yz, 8, HD), F32),
            pltpu.VMEM((n_yz, 8, HD), BF16),
            pltpu.VMEM((9, 2, 8, HD), BF16),
            pltpu.VMEM((9, 16, 8, HD), BF16),
            pltpu.SemaphoreType.REGULAR, dma((5,)), dma((3, 3)), dma((3, 3)), dma((3,)), dma((2,)), dma((7,)), dma((3, X)),
            dma, dma, dma((X,)), dma, dma((8, 3)), dma((2,)), dma((2,)), dma((2,)), dma((2,)),
            dma((3,)), dma((3,)), dma((3, 3)), dma((3, 3)), dma, dma, dma, dma, dma((3,)), dma((3,)), dma((4,)), dma((4,)),
        ],
        compiler_params=pltpu.CompilerParams(
            collective_id=0, has_side_effects=True, vmem_limit_bytes=60 * 1024 * 1024
        ),
        name="region_step",
    )(
        region_lengths,
        query_rows,
        key_rows,
        value_rows,
        norm_gain.reshape(HEADS, HD),
        conv_weight,
        cotangent,
    )
    return decoded, grad.reshape(9, 128, 128)


def solution(mesh):
    placed = (
        P("seq", "dp", None),
        P("seq", "dp", None),
        P("seq", "dp", None),
        P("dp"),
        P(),
        P(),
        P("dp", "seq", None, None),
    )
    return jax.shard_map(
        body,
        mesh=mesh,
        in_specs=placed,
        out_specs=(P("dp", "seq", None, None), P()),
        check_vma=False,
    )
```

```python
import functools
import math

import jax
import jax.numpy as jnp
from jax import lax
from jax.experimental import pallas as pl
from jax.experimental.pallas import tpu as pltpu
from jax.sharding import PartitionSpec as P

HEADS = 16
PATCH = 4
MESH = pl.DeviceIdType.MESH
X, Z = 4, 8
TOK, HD = 64, 128
OWNED = 18
F32, BF16 = jnp.float32, jnp.bfloat16


def remote(src, dst, send, recv, device):
    return pltpu.make_async_remote_copy(
        src_ref=src, dst_ref=dst, send_sem=send, recv_sem=recv, device_id=device, device_id_type=MESH
    )


def wait_bytes(ref, sem):
    pltpu.make_async_copy(ref, ref, sem).wait()


def step_kernel(n_dp, lens_ref, q_hbm, k_hbm, v_hbm, gain_ref, w_hbm, cot_hbm, dec_ref, wg_ref,
                raw, w_ref, cot_ref, cot_side, pairs, split, stage, rk, rq, rv, hold, probs, sums, o_mid, o_in, o_hold, att, ext, cot_t, grid, wide,
                taps, buf1, acc1, buf2, acc2, buf3, buf4, fin, whole,
                inside, load, sx, rx, sz, rz, rzq, rr, so, ro, rro, sx2, rx2, sh, rh, sc, rc,
                s1, r1, s2, r2, s3, r3, s4, r4, s5, r5, s6, r6):
    dp, seq = lax.axis_index("dp"), lax.axis_index("seq")
    n_seq = X * Z
    n_yz = (n_dp // 2) * Z
    core, z, x = dp % 2, seq // X, seq % X
    member = (dp // 2) * Z + z
    partner = (dp + 1 - 2 * core, seq)
    half = 2 + 4 * core

    def x_device(step):
        return (dp, z * X + (x + step) % X)

    def z_device(step):
        return (dp, ((z + step) % Z) * X + x)

    def yz_device(index):
        return ((index // Z) * 2 + core, (index % Z) * X + x)

    loads = [pltpu.make_async_copy(src, dst, load.at[i]) for i, (src, dst) in enumerate((
        (k_hbm, raw.at[0]), (q_hbm, raw.at[1]), (v_hbm, raw.at[2]), (cot_hbm, cot_ref), (w_hbm, w_ref)))]
    for copy in loads:
        copy.start()

    barrier = pltpu.get_barrier_semaphore()

    def signal(device):
        pl.semaphore_signal(barrier, inc=1, device_id=device, device_id_type=MESH)

    n_y = n_dp // 2

    def y_device(step):
        return (((dp // 2 + step) % n_y) * 2 + core, seq)

    for step in range(1, n_y):
        signal(y_device(step))
    for step in range(1, Z):
        signal(z_device(step))
    for step in range(1, X):
        signal(x_device(step))
    signal(partner)
    signal((dp, (seq + 1) % n_seq))
    signal((dp, (seq + n_seq - 1) % n_seq))

    def divide(array):
        loads[array].wait()
        for head in range(HEADS):
            both = raw[array, :, :, head * HD:(head + 1) * HD].astype(F32)
            pairs[head % 4] = both.reshape(2 * TOK, HD)
            for region in range(2):
                item = region * HEADS + head
                split[array, item // X, item % X] = pairs[head % 4, pl.ds(region, TOK, stride=2), :].astype(BF16)

    divide(0)
    pl.semaphore_wait(barrier, (n_y - 1) + (Z - 1) + (X - 1) + 1 + 2)

    landed = (rk, rq, rv)
    far_first = (4, 3, 5, 2, 6, 1, 7)

    x_copies = []

    def along_x(array):
        for step in (1, 3, 2):
            copy = remote(split.at[array, :, (x + step) % X], stage.at[array, :, x],
                          sx.at[array, step - 1], rx.at[array, step - 1], x_device(step))
            copy.start()
            x_copies.append(copy)

    def arrival(array, step):
        return (rz.at[0], rzq.at[step - 1], rz.at[1])[array]

    def along_z(array, blocks, column, step):
        block = blocks.at[(z + step) % Z, column]
        if step == 4:
            remote(block, hold.at[array, column], sz.at[array], rr.at[array, column], z_device(half)).start()
        else:
            remote(block, landed[array].at[z, column], sz.at[array], arrival(array, step), z_device(step)).start()

    others = [(x + X - step) % X for step in (1, 3, 2)]

    def came(array, number):
        wait_bytes(stage.at[array, :, others[number]], rx.at[array, (1, 3, 2)[number] - 1])
        landed[array][z, others[number]] = stage[array, z, others[number]]

    def onward(array, column):
        wait_bytes(hold.at[array, column], rr.at[array, column])
        remote(hold.at[array, column], landed[array].at[(z + Z - half) % Z, column], sz.at[array], arrival(array, 4),
               z_device(half)).start()

    for array in range(3):
        if array:
            divide(array)
        along_x(array)
        for step in far_first:
            along_z(array, split.at[array], x, step)
        landed[array][z, x] = split[array, z, x]

    for step in range(1, n_y):
        pl.semaphore_signal(inside, inc=1, device_id=y_device(step), device_id_type=MESH)

    loads[3].wait()
    loads[4].wait()

    def turn(row, first, second):
        grid[0], grid[1] = first.astype(F32), second.astype(F32)
        low = (row + 1) * 2 * TOK
        for px in range(PATCH):
            part = [grid[region, pl.ds(px, TOK, stride=PATCH), :] for region in range(2)]
            cot_t[px * HD:(px + 1) * HD, low:low + 2 * TOK] = jnp.concatenate(part).T.astype(BF16)

    for row in range(PATCH):
        turn(row, cot_ref[0, row], cot_ref[1, row])
    wide[...] = jnp.zeros_like(wide)
    for dy in range(3):
        for dx in range(3):
            for px in range(PATCH):
                wide[dy, (px + dx) * HD:(px + dx + 1) * HD, px * HD:(px + 1) * HD] = w_ref[3 * dy + dx]

    columns = [x] + others
    for number in range(3):
        came(0, number)
        for step in far_first:
            along_z(0, stage.at[0], others[number], step)
    for number in range(3):
        came(1, number)
    for step in far_first:
        for column in others:
            along_z(1, stage.at[1], column, step)
    for column in columns:
        onward(0, column)

    region_len = lens_ref[seq // HEADS]
    key_slot = lax.broadcasted_iota(jnp.int32, (1, n_seq * TOK), 1)
    bias = jnp.where(key_slot < region_len, 0.0, -1e30).astype(F32)
    factor = math.log2(math.e) / math.sqrt(HD)

    def powers(step):
        index = (z + Z - step) % Z
        if step:
            wait_bytes(rq.at[index], rzq.at[step - 1])
        query = rq[index].reshape(X * TOK, HD)
        keys = rk[...].reshape(n_seq * TOK, HD)
        scores = lax.dot_general(query, keys, (((1,), (1,)), ((), ())), preferred_element_type=F32) + bias
        top = jnp.max(scores, axis=1, keepdims=True)
        power = jnp.exp2((scores - top) * factor)
        sums[index] = jnp.sum(power, axis=1, keepdims=True)
        probs[index] = power.astype(BF16)

    wait_bytes(rk.at[pl.ds(0, Z - 1)], rz.at[0])
    powers(0)
    for number in range(3):
        came(2, number)
        for step in far_first:
            along_z(2, stage.at[2], others[number], step)
    for column in columns:
        onward(1, column)

    cot_down = remote(cot_ref.at[:, 3], cot_side.at[0], sc.at[0], rc.at[0], (dp, (seq + 1) % n_seq))
    cot_up = remote(cot_ref.at[:, 0], cot_side.at[1], sc.at[1], rc.at[1], (dp, (seq + n_seq - 1) % n_seq))

    @pl.when(x < X - 1)
    def _():
        cot_down.start()

    @pl.when(x > 0)
    def _():
        cot_up.start()

    powers(3)
    powers(5)
    powers(2)
    for column, step in zip(columns, (6, 1, 7)):
        powers(step)
        onward(2, column)
    onward(2, columns[3])
    powers(4)
    wait_bytes(rv.at[pl.ds(0, Z - 1)], rz.at[1])

    def mixed(step):
        to = (z + step) % Z
        out = jnp.dot(probs[to], rv[...].reshape(n_seq * TOK, HD), preferred_element_type=F32) / sums[to]
        o_mid[to] = out.astype(BF16).reshape(X, TOK, HD)

    def home(blocks, column, step):
        block = blocks.at[(z + step) % Z, column]
        if step == 4:
            remote(block, o_hold.at[column], so, rro.at[column], z_device(half)).start()
        else:
            remote(block, att.at[z, column], so, ro, z_device(step)).start()

    for step in far_first + (0,):
        mixed(step)
        to = (z + step) % Z
        for side in (2, 1, 3):
            block = o_mid.at[to, (x + side) % X]
            if step:
                remote(block, o_in.at[to, x], sx2, rx2.at[step - 1, side - 1], x_device(side)).start()
            else:
                remote(block, att.at[z, x], sx2, rx2.at[7, side - 1], x_device(side)).start()
        if step:
            home(o_mid, x, step)
    att[z, x] = o_mid[z, x]

    @pl.when(jnp.logical_and(x == X - 1, seq < n_seq - 1))
    def _():
        cot_down.start()

    @pl.when(jnp.logical_and(x == 0, seq > 0))
    def _():
        cot_up.start()

    def passing(step):
        for side in (1, 3, 2):
            column = (x + X - side) % X
            wait_bytes(o_in.at[(z + step) % Z, column], rx2.at[step - 1, side - 1])
            home(o_in, column, step)

    for step in (4, 3, 5, 2, 6):
        passing(step)
    for column in columns:
        wait_bytes(o_hold.at[column], rro.at[column])
        remote(o_hold.at[column], att.at[(z + Z - half) % Z, column], so, ro, z_device(half)).start()
    for step in (1, 7):
        passing(step)
    @pl.when(seq < n_seq - 1)
    def _():
        cot_down.wait_send()
        wait_bytes(cot_side.at[1], rc.at[1])

    @pl.when(seq > 0)
    def _():
        cot_up.wait_send()
        wait_bytes(cot_side.at[0], rc.at[0])

    @pl.when(seq == 0)
    def _():
        cot_side[0] = jnp.zeros((2, PATCH * TOK, HD), BF16)

    @pl.when(seq == n_seq - 1)
    def _():
        cot_side[1] = jnp.zeros((2, PATCH * TOK, HD), BF16)

    turn(PATCH, cot_side[1, 0], cot_side[1, 1])
    turn(-1, cot_side[0, 0], cot_side[0, 1])
    for side in range(1, X):
        wait_bytes(att.at[z, (x + X - side) % X], rx2.at[7, side - 1])
    wait_bytes(att.at[pl.ds(0, Z - 1)], ro)

    row_of = lax.broadcasted_iota(jnp.int32, (TOK, HD), 0)

    def put_sides(row, region, first, last):
        rows = pl.ds(region * TOK, TOK)
        before = jnp.where(row_of == 0, 0.0, pltpu.roll(last, 1, 0))
        after = jnp.where(row_of == TOK - 1, 0.0, pltpu.roll(first, TOK - 1, 0))
        ext[row, rows, 0:HD] = before.astype(BF16)
        ext[row, rows, 5 * HD:6 * HD] = after.astype(BF16)

    for region in range(2):
        values = att[4 * region:4 * region + 4].astype(F32)
        count = 1.0 / (HEADS * HD)
        mean = jnp.sum(jnp.sum(values, axis=(0, 1)), axis=1, keepdims=True) * count
        centered = values - mean
        var = jnp.sum(jnp.sum(centered * centered, axis=(0, 1)), axis=1, keepdims=True) * count
        scale = lax.rsqrt(var + 1e-05)
        live = seq * TOK + row_of < lens_ref[region]
        for py in range(PATCH):
            line = []
            for px in range(PATCH):
                head = PATCH * py + px
                normed = centered[py, px] * scale * gain_ref[head:head + 1, :]
                normed = jnp.where(live, normed, 0.0)
                ext[py + 1, region * TOK:(region + 1) * TOK, (px + 1) * HD:(px + 2) * HD] = normed.astype(BF16)
                line.append(normed)
            put_sides(py + 1, region, line[0], line[3])

    middle = pl.ds(HD, PATCH * HD)
    down = remote(ext.at[4, :, middle], ext.at[0, :, middle], sh.at[0], rh.at[0], (dp, (seq + 1) % n_seq))
    up = remote(ext.at[1, :, middle], ext.at[5, :, middle], sh.at[1], rh.at[1], (dp, (seq + n_seq - 1) % n_seq))

    def lines(low, high):
        return ext[low:high].reshape((high - low) * 2 * TOK, 6 * HD)

    def taps_of(dy):
        low = (2 - dy) * 2 * TOK
        rows = ext[1:5].reshape(PATCH * 2 * TOK, 6 * HD)
        blocks = [
            jnp.dot(cot_t[pair * HD:(pair + 2) * HD, low:low + PATCH * 2 * TOK], rows[:, pair * HD:(pair + 4) * HD],
                    preferred_element_type=F32)
            for pair in (0, 2)
        ]
        for dx in range(3):
            total = None
            for block in blocks:
                for px in range(2):
                    part = block[px * HD:(px + 1) * HD, (px + dx) * HD:(px + dx + 1) * HD]
                    total = part if total is None else total + part
            taps[3 * dy + dx] = total.T.reshape(16, 8, HD)

    def three(ref, dy, *rest):
        return ref.at[(pl.ds(3 * dy, 3),) + rest]

    def to_core(dy):
        return remote(three(taps, dy, pl.ds(8 * (1 - core), 8)), three(buf1, dy), s1.at[dy], r1.at[dy], partner)

    def to_x(dy, step):
        return remote(three(acc1, dy, pl.ds(2 * ((x + step) % X), 2)), buf2.at[step - 1, pl.ds(3 * dy, 3)],
                      s2.at[dy, step - 1], r2.at[dy, step - 1], x_device(step))

    def cores_done(dy):
        to_core(dy).wait()
        some = slice(3 * dy, 3 * dy + 3)
        acc1[some] = taps[some, pl.ds(8 * core, 8)] + buf1[some]
        for step in (2, 1, 3):
            to_x(dy, step).start()

    taps_of(1)
    to_core(1).start()

    taps_of(0)
    to_core(0).start()
    cores_done(1)
    taps_of(2)
    to_core(2).start()
    cores_done(0)
    cores_done(2)

    @pl.when(seq < n_seq - 1)
    def _():
        down.start()

    @pl.when(seq > 0)
    def _():
        up.start()

    pl.semaphore_wait(inside, n_y - 1)
    for dy in (1, 0, 2):
        for step in range(1, X):
            to_x(dy, step).wait()
        some = slice(3 * dy, 3 * dy + 3)
        acc2[some] = (acc1[some, pl.ds(2 * x, 2)] + buf2[0, some]) + (buf2[1, some] + buf2[2, some])
        for tile in range(6 * dy, 6 * dy + 6):
            owner = (3 * tile + core) % n_yz

            @pl.when(owner != member)
            def _():
                remote(acc2.at[tile // 2, tile % 2], buf3.at[member], s3, r3, yz_device(owner)).start()
    offset = (member + n_yz - core) % n_yz

    @pl.when(seq < n_seq - 1)
    def _():
        down.wait_send()
        wait_bytes(ext.at[5, :, middle], rh.at[1])

    @pl.when(seq > 0)
    def _():
        up.wait_send()
        wait_bytes(ext.at[0, :, middle], rh.at[0])

    @pl.when(seq == 0)
    def _():
        ext[0] = jnp.zeros((2 * TOK, 6 * HD), BF16)

    @pl.when(seq == n_seq - 1)
    def _():
        ext[5] = jnp.zeros((2 * TOK, 6 * HD), BF16)

    for row in (0, 5):
        for region in range(2):
            rows = pl.ds(region * TOK, TOK)
            put_sides(row, region, ext[row, rows, HD:2 * HD].astype(F32), ext[row, rows, 4 * HD:5 * HD].astype(F32))

    decoded = jnp.dot(lines(0, 4), wide[0], preferred_element_type=F32)
    decoded += jnp.dot(lines(1, 5), wide[1], preferred_element_type=F32)
    decoded += jnp.dot(lines(2, 6), wide[2], preferred_element_type=F32)
    for row in range(PATCH):
        for region in range(2):
            low = (row * 2 + region) * TOK
            for px in range(PATCH):
                grid[region, pl.ds(px, TOK, stride=PATCH), :] = decoded[low:low + TOK, px * HD:(px + 1) * HD]
            dec_ref[region, row] = grid[region].astype(BF16)

    mine = offset // 3
    owns = jnp.logical_and(offset % 3 == 0, mine < OWNED)
    away = [(dy, dz) for dy in range(n_y) for dz in range(Z) if dy or dz]
    away.sort(key=lambda d: -min(d[0], n_y - d[0]) - min(d[1], Z - d[1]))

    @pl.when(owns)
    def _():
        wait_bytes(buf3.at[pl.ds(0, n_yz - 1)], r3)
        buf3[member] = acc2[mine // 2, mine % 2]
        total = jnp.sum(buf3[...], axis=0) * (1.0 / math.sqrt(PATCH * PATCH * TOK))
        fin[mine // 2, mine % 2] = total.astype(BF16)
        part = fin.at[mine // 2, mine % 2]
        for dy, dz in away:
            device = (((dp // 2 + dy) % n_y) * 2 + core, ((z + dz) % Z) * X + x)
            remote(part, part, s4, r4.at[mine // 6], device).start()

    def place(dy, which):
        return whole.at[pl.ds(3 * dy, 3), pl.ds(8 * core + 2 * which, 2)]

    def back_x(dy, step):
        return remote(three(fin, dy), place(dy, x), s5.at[dy, step - 1], r5.at[dy, step - 1], x_device(step))

    def back_core(dy, number, src, which):
        return remote(src, place(dy, which), s6.at[dy, number], r6.at[dy, number], partner)

    forwards = []
    for dy in (1, 0, 2):
        owned_here = jnp.logical_and(owns, mine // 6 == dy)

        @pl.when(owned_here)
        def _():
            wait_bytes(buf4.at[pl.ds(0, 5)], r4.at[dy])

        @pl.when(jnp.logical_not(owned_here))
        def _():
            wait_bytes(buf4.at[pl.ds(0, 6)], r4.at[dy])

        for step in (1, 3, 2):
            back_x(dy, step).start()
        forwards.append(back_core(dy, 0, three(fin, dy), x))
        forwards[-1].start()
        whole[3 * dy:3 * dy + 3, pl.ds(8 * core + 2 * x, 2)] = fin[3 * dy:3 * dy + 3]
    for dy in (1, 0, 2):
        for step in (1, 3, 2):
            back_x(dy, step).wait()
            which = (x + X - step) % X
            forwards.append(back_core(dy, step, place(dy, which), which))
            forwards[-1].start()

    @pl.when(owns)
    def _():
        wait_bytes(buf3.at[pl.ds(0, OWNED - 1)], s3)
        wait_bytes(buf4.at[pl.ds(0, n_yz - 1)], s4)

    @pl.when(jnp.logical_not(owns))
    def _():
        wait_bytes(buf3.at[pl.ds(0, OWNED)], s3)

    for copy in x_copies:
        copy.wait_send()
    for array in range(3):
        wait_bytes(landed[array], sz.at[array])
    wait_bytes(o_in, so)
    wait_bytes(att.at[pl.ds(0, 6)], sx2)
    for forward in forwards:
        forward.wait()
    wg_ref[...] = whole[...].astype(F32)


def results_kernel(decoded_ref, grad_ref, decoded_out, grad_out, sems):
    copies = [pltpu.make_async_copy(decoded_ref, decoded_out, sems.at[0]),
              pltpu.make_async_copy(grad_ref, grad_out, sems.at[1])]
    for copy in copies:
        copy.start()
    for copy in copies:
        copy.wait()


def body(query_rows, key_rows, value_rows, region_lengths, norm_gain, conv_weight, cotangent):
    n_dp = lax.axis_size("dp")
    n_yz = (n_dp // 2) * Z
    hbm = pl.BlockSpec(memory_space=pl.ANY)
    vmem = pl.BlockSpec(memory_space=pltpu.VMEM)
    dma = pltpu.SemaphoreType.DMA
    decoded, grad = pl.pallas_call(
        functools.partial(step_kernel, n_dp),
        out_shape=(pltpu.VMEM((2, 4, 256, 128), BF16), pltpu.VMEM((9, 16, 8, 128), F32)),
        in_specs=[pl.BlockSpec(memory_space=pltpu.SMEM), hbm, hbm, hbm, vmem, hbm, hbm],
        out_specs=(vmem, vmem),
        scratch_shapes=[
            pltpu.VMEM((3, TOK, 2, HEADS * HD), BF16),
            pltpu.VMEM((9, HD, HD), BF16),
            pltpu.VMEM((2, PATCH, PATCH * TOK, HD), BF16),
            pltpu.VMEM((2, 2, PATCH * TOK, HD), BF16),
            pltpu.VMEM((4, 2 * TOK, HD), F32),
            pltpu.VMEM((3, Z, X, TOK, HD), BF16),
            pltpu.VMEM((3, Z, X, TOK, HD), BF16),
            pltpu.VMEM((Z, X, TOK, HD), BF16),
            pltpu.VMEM((Z, X, TOK, HD), BF16),
            pltpu.VMEM((Z, X, TOK, HD), BF16),
            pltpu.VMEM((3, X, TOK, HD), BF16),
            pltpu.VMEM((Z, X * TOK, X * Z * TOK), BF16),
            pltpu.VMEM((Z, X * TOK, 1), F32),
            pltpu.VMEM((Z, X, TOK, HD), BF16),
            pltpu.VMEM((Z, X, TOK, HD), BF16),
            pltpu.VMEM((X, TOK, HD), BF16),
            pltpu.VMEM((Z, X, TOK, HD), BF16),
            pltpu.VMEM((6, 2 * TOK, 6 * HD), BF16),
            pltpu.VMEM((4 * HD, 6 * 2 * TOK), BF16),
            pltpu.VMEM((2, PATCH * TOK, HD), F32),
            pltpu.VMEM((3, 6 * HD, 4 * HD), BF16),
            pltpu.VMEM((9, 16, 8, HD), F32),
            pltpu.VMEM((9, 8, 8, HD), F32),
            pltpu.VMEM((9, 8, 8, HD), F32),
            pltpu.VMEM((3, 9, 2, 8, HD), F32),
            pltpu.VMEM((9, 2, 8, HD), F32),
            pltpu.VMEM((n_yz, 8, HD), F32),
            pltpu.VMEM((n_yz, 8, HD), BF16),
            pltpu.VMEM((9, 2, 8, HD), BF16),
            pltpu.VMEM((9, 16, 8, HD), BF16),
            pltpu.SemaphoreType.REGULAR, dma((5,)), dma((3, 3)), dma((3, 3)), dma((3,)), dma((2,)), dma((7,)), dma((3, X)),
            dma, dma, dma((X,)), dma, dma((8, 3)), dma((2,)), dma((2,)), dma((2,)), dma((2,)),
            dma((3,)), dma((3,)), dma((3, 3)), dma((3, 3)), dma, dma, dma, dma((3,)), dma((3, 3)), dma((3, 3)), dma((3, 4)), dma((3, 4)),
        ],
        compiler_params=pltpu.CompilerParams(
            collective_id=0, has_side_effects=True, vmem_limit_bytes=60 * 1024 * 1024
        ),
        name="region_step",
    )(
        region_lengths,
        query_rows,
        key_rows,
        value_rows,
        norm_gain.reshape(HEADS, HD),
        conv_weight,
        cotangent,
    )
    return pl.pallas_call(
        results_kernel,
        out_shape=(jax.ShapeDtypeStruct((2, 4, 256, 128), BF16), jax.ShapeDtypeStruct((9, 128, 128), F32)),
        in_specs=[hbm, hbm],
        out_specs=(hbm, hbm),
        scratch_shapes=[dma((2,))],
        compiler_params=pltpu.CompilerParams(vmem_limit_bytes=2 * 1024 * 1024),
        name="results",
    )(decoded, grad.reshape(9, 128, 128))


def solution(mesh):
    placed = (
        P("seq", "dp", None),
        P("seq", "dp", None),
        P("seq", "dp", None),
        P("dp"),
        P(),
        P(),
        P("dp", "seq", None, None),
    )
    return jax.shard_map(
        body,
        mesh=mesh,
        in_specs=placed,
        out_specs=(P("dp", "seq", None, None), P()),
        check_vma=False,
    )
```

```python
import functools
import math

import jax
import jax.numpy as jnp
from jax import lax
from jax.experimental import pallas as pl
from jax.experimental.pallas import tpu as pltpu
from jax.sharding import PartitionSpec as P

HEADS = 16
PATCH = 4
MESH = pl.DeviceIdType.MESH
X, Z = 4, 8
TOK, HD = 64, 128
OWNED = 18
F32, BF16 = jnp.float32, jnp.bfloat16


def remote(src, dst, send, recv, device):
    return pltpu.make_async_remote_copy(
        src_ref=src, dst_ref=dst, send_sem=send, recv_sem=recv, device_id=device, device_id_type=MESH
    )


def wait_bytes(ref, sem):
    pltpu.make_async_copy(ref, ref, sem).wait()


def step_kernel(n_dp, lens_ref, q_hbm, k_hbm, v_hbm, gain_ref, w_hbm, cot_hbm, dec_ref, wg_ref,
                raw, w_ref, cot_ref, cot_side, pairs, split, stage, rk, rq, rv, hold, probs, sums, o_mid, o_in, o_hold, att, ext, cot_t, grid, wide,
                taps, buf1, acc1, buf2, acc2, buf3, buf4, fin, whole,
                inside, load, sx, rx, sz, rz, rzq, rr, so, ro, rro, sx2, rx2, sh, rh, sc, rc,
                s1, r1, s2, r2, s3, r3, s4, r4, s5, r5, s6, r6):
    dp, seq = lax.axis_index("dp"), lax.axis_index("seq")
    n_seq = X * Z
    n_yz = (n_dp // 2) * Z
    core, z, x = dp % 2, seq // X, seq % X
    member = (dp // 2) * Z + z
    partner = (dp + 1 - 2 * core, seq)
    half = 2 + 4 * core

    def x_device(step):
        return (dp, z * X + (x + step) % X)

    def z_device(step):
        return (dp, ((z + step) % Z) * X + x)

    def yz_device(index):
        return ((index // Z) * 2 + core, (index % Z) * X + x)

    loads = [pltpu.make_async_copy(src, dst, load.at[i]) for i, (src, dst) in enumerate((
        (k_hbm, raw.at[0]), (q_hbm, raw.at[1]), (v_hbm, raw.at[2]), (cot_hbm, cot_ref), (w_hbm, w_ref)))]
    loads[0].start()

    barrier = pltpu.get_barrier_semaphore()

    def signal(device):
        pl.semaphore_signal(barrier, inc=1, device_id=device, device_id_type=MESH)

    n_y = n_dp // 2

    def y_device(step):
        return (((dp // 2 + step) % n_y) * 2 + core, seq)

    for step in range(1, n_y):
        signal(y_device(step))
    for step in range(1, Z):
        signal(z_device(step))
    for step in range(1, X):
        signal(x_device(step))
    signal(partner)
    signal((dp, (seq + 1) % n_seq))
    signal((dp, (seq + n_seq - 1) % n_seq))

    def divide(array):
        loads[array].wait()
        if array == 0:
            for copy in loads[1:]:
                copy.start()
        for head in range(HEADS):
            both = raw[array, :, :, head * HD:(head + 1) * HD].astype(F32)
            pairs[head % 4] = both.reshape(2 * TOK, HD)
            for region in range(2):
                item = region * HEADS + head
                split[array, item // X, item % X] = pairs[head % 4, pl.ds(region, TOK, stride=2), :].astype(BF16)

    divide(0)
    pl.semaphore_wait(barrier, (n_y - 1) + (Z - 1) + (X - 1) + 1 + 2)

    landed = (rk, rq, rv)
    far_first = (4, 3, 5, 2, 6, 1, 7)

    x_copies = []

    def along_x(array):
        for step in (1, 3, 2):
            copy = remote(split.at[array, :, (x + step) % X], stage.at[array, :, x],
                          sx.at[array, step - 1], rx.at[array, step - 1], x_device(step))
            copy.start()
            x_copies.append(copy)

    def arrival(array, step):
        return (rz.at[0], rzq.at[step - 1], rz.at[1])[array]

    def along_z(array, blocks, column, step):
        block = blocks.at[(z + step) % Z, column]
        if step == 4:
            remote(block, hold.at[array, column], sz.at[array], rr.at[array, column], z_device(half)).start()
        else:
            remote(block, landed[array].at[z, column], sz.at[array], arrival(array, step), z_device(step)).start()

    others = [(x + X - step) % X for step in (1, 3, 2)]

    def came(array, number):
        wait_bytes(stage.at[array, :, others[number]], rx.at[array, (1, 3, 2)[number] - 1])
        landed[array][z, others[number]] = stage[array, z, others[number]]

    def onward(array, column):
        wait_bytes(hold.at[array, column], rr.at[array, column])
        remote(hold.at[array, column], landed[array].at[(z + Z - half) % Z, column], sz.at[array], arrival(array, 4),
               z_device(half)).start()

    for array in range(3):
        if array:
            divide(array)
        along_x(array)
        for step in far_first:
            along_z(array, split.at[array], x, step)
        landed[array][z, x] = split[array, z, x]

    for step in range(1, n_y):
        pl.semaphore_signal(inside, inc=1, device_id=y_device(step), device_id_type=MESH)

    loads[3].wait()
    loads[4].wait()

    def turn(row, first, second):
        grid[0], grid[1] = first.astype(F32), second.astype(F32)
        low = (row + 1) * 2 * TOK
        for px in range(PATCH):
            part = [grid[region, pl.ds(px, TOK, stride=PATCH), :] for region in range(2)]
            cot_t[px * HD:(px + 1) * HD, low:low + 2 * TOK] = jnp.concatenate(part).T.astype(BF16)

    for row in range(PATCH):
        turn(row, cot_ref[0, row], cot_ref[1, row])
    wide[...] = jnp.zeros_like(wide)
    for dy in range(3):
        for dx in range(3):
            for px in range(PATCH):
                wide[dy, (px + dx) * HD:(px + dx + 1) * HD, px * HD:(px + 1) * HD] = w_ref[3 * dy + dx]

    columns = [x] + others
    for number in range(3):
        came(0, number)
        for step in far_first:
            along_z(0, stage.at[0], others[number], step)
    for number in range(3):
        came(1, number)
    for step in far_first:
        for column in others:
            along_z(1, stage.at[1], column, step)
    for column in columns:
        onward(0, column)

    region_len = lens_ref[seq // HEADS]
    key_slot = lax.broadcasted_iota(jnp.int32, (1, n_seq * TOK), 1)
    bias = jnp.where(key_slot < region_len, 0.0, -1e30).astype(F32)
    factor = math.log2(math.e) / math.sqrt(HD)

    def powers(step):
        index = (z + Z - step) % Z
        if step:
            wait_bytes(rq.at[index], rzq.at[step - 1])
        query = rq[index].reshape(X * TOK, HD)
        keys = rk[...].reshape(n_seq * TOK, HD)
        scores = lax.dot_general(query, keys, (((1,), (1,)), ((), ())), preferred_element_type=F32) + bias
        top = jnp.max(scores, axis=1, keepdims=True)
        power = jnp.exp2((scores - top) * factor)
        sums[index] = jnp.sum(power, axis=1, keepdims=True)
        probs[index] = power.astype(BF16)

    wait_bytes(rk.at[pl.ds(0, Z - 1)], rz.at[0])
    powers(0)
    for number in range(3):
        came(2, number)
        for step in far_first:
            along_z(2, stage.at[2], others[number], step)
    for column in columns:
        onward(1, column)

    cot_down = remote(cot_ref.at[:, 3], cot_side.at[0], sc.at[0], rc.at[0], (dp, (seq + 1) % n_seq))
    cot_up = remote(cot_ref.at[:, 0], cot_side.at[1], sc.at[1], rc.at[1], (dp, (seq + n_seq - 1) % n_seq))

    @pl.when(x < X - 1)
    def _():
        cot_down.start()

    @pl.when(x > 0)
    def _():
        cot_up.start()

    powers(3)
    powers(5)
    powers(2)
    for column, step in zip(columns, (6, 1, 7)):
        powers(step)
        onward(2, column)
    onward(2, columns[3])
    powers(4)
    wait_bytes(rv.at[pl.ds(0, Z - 1)], rz.at[1])

    def mixed(step):
        to = (z + step) % Z
        out = jnp.dot(probs[to], rv[...].reshape(n_seq * TOK, HD), preferred_element_type=F32) / sums[to]
        o_mid[to] = out.astype(BF16).reshape(X, TOK, HD)

    def home(blocks, column, step):
        block = blocks.at[(z + step) % Z, column]
        if step == 4:
            remote(block, o_hold.at[column], so, rro.at[column], z_device(half)).start()
        else:
            remote(block, att.at[z, column], so, ro, z_device(step)).start()

    for step in far_first + (0,):
        mixed(step)
        to = (z + step) % Z
        for side in (2, 1, 3):
            block = o_mid.at[to, (x + side) % X]
            if step:
                remote(block, o_in.at[to, x], sx2, rx2.at[step - 1, side - 1], x_device(side)).start()
            else:
                remote(block, att.at[z, x], sx2, rx2.at[7, side - 1], x_device(side)).start()
        if step:
            home(o_mid, x, step)
    att[z, x] = o_mid[z, x]

    @pl.when(jnp.logical_and(x == X - 1, seq < n_seq - 1))
    def _():
        cot_down.start()

    @pl.when(jnp.logical_and(x == 0, seq > 0))
    def _():
        cot_up.start()

    def passing(step):
        for side in (1, 3, 2):
            column = (x + X - side) % X
            wait_bytes(o_in.at[(z + step) % Z, column], rx2.at[step - 1, side - 1])
            home(o_in, column, step)

    for step in (4, 3, 5, 2, 6):
        passing(step)
    for column in columns:
        wait_bytes(o_hold.at[column], rro.at[column])
        remote(o_hold.at[column], att.at[(z + Z - half) % Z, column], so, ro, z_device(half)).start()
    for step in (1, 7):
        passing(step)
    @pl.when(seq < n_seq - 1)
    def _():
        cot_down.wait_send()
        wait_bytes(cot_side.at[1], rc.at[1])

    @pl.when(seq > 0)
    def _():
        cot_up.wait_send()
        wait_bytes(cot_side.at[0], rc.at[0])

    @pl.when(seq == 0)
    def _():
        cot_side[0] = jnp.zeros((2, PATCH * TOK, HD), BF16)

    @pl.when(seq == n_seq - 1)
    def _():
        cot_side[1] = jnp.zeros((2, PATCH * TOK, HD), BF16)

    turn(PATCH, cot_side[1, 0], cot_side[1, 1])
    turn(-1, cot_side[0, 0], cot_side[0, 1])
    for side in range(1, X):
        wait_bytes(att.at[z, (x + X - side) % X], rx2.at[7, side - 1])
    wait_bytes(att.at[pl.ds(0, Z - 1)], ro)

    row_of = lax.broadcasted_iota(jnp.int32, (TOK, HD), 0)

    def put_sides(row, region, first, last):
        rows = pl.ds(region * TOK, TOK)
        before = jnp.where(row_of == 0, 0.0, pltpu.roll(last, 1, 0))
        after = jnp.where(row_of == TOK - 1, 0.0, pltpu.roll(first, TOK - 1, 0))
        ext[row, rows, 0:HD] = before.astype(BF16)
        ext[row, rows, 5 * HD:6 * HD] = after.astype(BF16)

    for region in range(2):
        values = att[4 * region:4 * region + 4].astype(F32)
        count = 1.0 / (HEADS * HD)
        mean = jnp.sum(jnp.sum(values, axis=(0, 1)), axis=1, keepdims=True) * count
        centered = values - mean
        var = jnp.sum(jnp.sum(centered * centered, axis=(0, 1)), axis=1, keepdims=True) * count
        scale = lax.rsqrt(var + 1e-05)
        live = seq * TOK + row_of < lens_ref[region]
        for py in range(PATCH):
            line = []
            for px in range(PATCH):
                head = PATCH * py + px
                normed = centered[py, px] * scale * gain_ref[head:head + 1, :]
                normed = jnp.where(live, normed, 0.0)
                ext[py + 1, region * TOK:(region + 1) * TOK, (px + 1) * HD:(px + 2) * HD] = normed.astype(BF16)
                line.append(normed)
            put_sides(py + 1, region, line[0], line[3])

    middle = pl.ds(HD, PATCH * HD)
    down = remote(ext.at[4, :, middle], ext.at[0, :, middle], sh.at[0], rh.at[0], (dp, (seq + 1) % n_seq))
    up = remote(ext.at[1, :, middle], ext.at[5, :, middle], sh.at[1], rh.at[1], (dp, (seq + n_seq - 1) % n_seq))

    def lines(low, high):
        return ext[low:high].reshape((high - low) * 2 * TOK, 6 * HD)

    def taps_of(dy):
        low = (2 - dy) * 2 * TOK
        rows = ext[1:5].reshape(PATCH * 2 * TOK, 6 * HD)
        blocks = [
            jnp.dot(cot_t[pair * HD:(pair + 2) * HD, low:low + PATCH * 2 * TOK], rows[:, pair * HD:(pair + 4) * HD],
                    preferred_element_type=F32)
            for pair in (0, 2)
        ]
        for dx in range(3):
            total = None
            for block in blocks:
                for px in range(2):
                    part = block[px * HD:(px + 1) * HD, (px + dx) * HD:(px + dx + 1) * HD]
                    total = part if total is None else total + part
            taps[3 * dy + dx] = total.T.reshape(16, 8, HD)

    def three(ref, dy, *rest):
        return ref.at[(pl.ds(3 * dy, 3),) + rest]

    def to_core(dy):
        return remote(three(taps, dy, pl.ds(8 * (1 - core), 8)), three(buf1, dy), s1.at[dy], r1.at[dy], partner)

    def to_x(dy, step):
        return remote(three(acc1, dy, pl.ds(2 * ((x + step) % X), 2)), buf2.at[step - 1, pl.ds(3 * dy, 3)],
                      s2.at[dy, step - 1], r2.at[dy, step - 1], x_device(step))

    def cores_done(dy):
        to_core(dy).wait()
        some = slice(3 * dy, 3 * dy + 3)
        acc1[some] = taps[some, pl.ds(8 * core, 8)] + buf1[some]
        for step in (2, 1, 3):
            to_x(dy, step).start()

    taps_of(1)
    to_core(1).start()

    taps_of(0)
    to_core(0).start()
    cores_done(1)
    taps_of(2)
    to_core(2).start()
    cores_done(0)
    cores_done(2)

    @pl.when(seq < n_seq - 1)
    def _():
        down.start()

    @pl.when(seq > 0)
    def _():
        up.start()

    pl.semaphore_wait(inside, n_y - 1)
    for dy in (1, 0, 2):
        for step in range(1, X):
            to_x(dy, step).wait()
        some = slice(3 * dy, 3 * dy + 3)
        acc2[some] = (acc1[some, pl.ds(2 * x, 2)] + buf2[0, some]) + (buf2[1, some] + buf2[2, some])
        for tile in range(6 * dy, 6 * dy + 6):
            owner = (3 * tile + core) % n_yz

            @pl.when(owner != member)
            def _():
                remote(acc2.at[tile // 2, tile % 2], buf3.at[member], s3, r3, yz_device(owner)).start()
    offset = (member + n_yz - core) % n_yz

    @pl.when(seq < n_seq - 1)
    def _():
        down.wait_send()
        wait_bytes(ext.at[5, :, middle], rh.at[1])

    @pl.when(seq > 0)
    def _():
        up.wait_send()
        wait_bytes(ext.at[0, :, middle], rh.at[0])

    @pl.when(seq == 0)
    def _():
        ext[0] = jnp.zeros((2 * TOK, 6 * HD), BF16)

    @pl.when(seq == n_seq - 1)
    def _():
        ext[5] = jnp.zeros((2 * TOK, 6 * HD), BF16)

    for row in (0, 5):
        for region in range(2):
            rows = pl.ds(region * TOK, TOK)
            put_sides(row, region, ext[row, rows, HD:2 * HD].astype(F32), ext[row, rows, 4 * HD:5 * HD].astype(F32))

    decoded = jnp.dot(lines(0, 4), wide[0], preferred_element_type=F32)
    decoded += jnp.dot(lines(1, 5), wide[1], preferred_element_type=F32)
    decoded += jnp.dot(lines(2, 6), wide[2], preferred_element_type=F32)
    for row in range(PATCH):
        for region in range(2):
            low = (row * 2 + region) * TOK
            for px in range(PATCH):
                grid[region, pl.ds(px, TOK, stride=PATCH), :] = decoded[low:low + TOK, px * HD:(px + 1) * HD]
            dec_ref[region, row] = grid[region].astype(BF16)

    mine = offset // 3
    owns = jnp.logical_and(offset % 3 == 0, mine < OWNED)
    away = [(dy, dz) for dy in range(n_y) for dz in range(Z) if dy or dz]
    away.sort(key=lambda d: -min(d[0], n_y - d[0]) - min(d[1], Z - d[1]))

    @pl.when(owns)
    def _():
        wait_bytes(buf3.at[pl.ds(0, n_yz - 1)], r3)
        buf3[member] = acc2[mine // 2, mine % 2]
        total = jnp.sum(buf3[...], axis=0) * (1.0 / math.sqrt(PATCH * PATCH * TOK))
        fin[mine // 2, mine % 2] = total.astype(BF16)
        part = fin.at[mine // 2, mine % 2]
        for dy, dz in away:
            device = (((dp // 2 + dy) % n_y) * 2 + core, ((z + dz) % Z) * X + x)
            remote(part, part, s4, r4.at[mine // 6], device).start()

    def place(dy, which):
        return whole.at[pl.ds(3 * dy, 3), pl.ds(8 * core + 2 * which, 2)]

    def back_x(dy, step):
        return remote(three(fin, dy), place(dy, x), s5.at[dy, step - 1], r5.at[dy, step - 1], x_device(step))

    def back_core(dy, number, src, which):
        return remote(src, place(dy, which), s6.at[dy, number], r6.at[dy, number], partner)

    forwards = []
    for dy in (1, 0, 2):
        owned_here = jnp.logical_and(owns, mine // 6 == dy)

        @pl.when(owned_here)
        def _():
            wait_bytes(buf4.at[pl.ds(0, 5)], r4.at[dy])

        @pl.when(jnp.logical_not(owned_here))
        def _():
            wait_bytes(buf4.at[pl.ds(0, 6)], r4.at[dy])

        for step in (1, 3, 2):
            back_x(dy, step).start()
        forwards.append(back_core(dy, 0, three(fin, dy), x))
        forwards[-1].start()
        whole[3 * dy:3 * dy + 3, pl.ds(8 * core + 2 * x, 2)] = fin[3 * dy:3 * dy + 3]
    for dy in (1, 0, 2):
        for step in (1, 3, 2):
            back_x(dy, step).wait()
            which = (x + X - step) % X
            forwards.append(back_core(dy, step, place(dy, which), which))
            forwards[-1].start()

    @pl.when(owns)
    def _():
        wait_bytes(buf3.at[pl.ds(0, OWNED - 1)], s3)
        wait_bytes(buf4.at[pl.ds(0, n_yz - 1)], s4)

    @pl.when(jnp.logical_not(owns))
    def _():
        wait_bytes(buf3.at[pl.ds(0, OWNED)], s3)

    for copy in x_copies:
        copy.wait_send()
    for array in range(3):
        wait_bytes(landed[array], sz.at[array])
    wait_bytes(o_in, so)
    wait_bytes(att.at[pl.ds(0, 6)], sx2)
    for forward in forwards:
        forward.wait()
    wg_ref[...] = whole[...].astype(F32)


def results_kernel(decoded_ref, grad_ref, decoded_out, grad_out, sems):
    copies = [pltpu.make_async_copy(decoded_ref, decoded_out, sems.at[0]),
              pltpu.make_async_copy(grad_ref, grad_out, sems.at[1])]
    for copy in copies:
        copy.start()
    for copy in copies:
        copy.wait()


def body(query_rows, key_rows, value_rows, region_lengths, norm_gain, conv_weight, cotangent):
    n_dp = lax.axis_size("dp")
    n_yz = (n_dp // 2) * Z
    hbm = pl.BlockSpec(memory_space=pl.ANY)
    vmem = pl.BlockSpec(memory_space=pltpu.VMEM)
    dma = pltpu.SemaphoreType.DMA
    decoded, grad = pl.pallas_call(
        functools.partial(step_kernel, n_dp),
        out_shape=(pltpu.VMEM((2, 4, 256, 128), BF16), pltpu.VMEM((9, 16, 8, 128), F32)),
        in_specs=[pl.BlockSpec(memory_space=pltpu.SMEM), hbm, hbm, hbm, vmem, hbm, hbm],
        out_specs=(vmem, vmem),
        scratch_shapes=[
            pltpu.VMEM((3, TOK, 2, HEADS * HD), BF16),
            pltpu.VMEM((9, HD, HD), BF16),
            pltpu.VMEM((2, PATCH, PATCH * TOK, HD), BF16),
            pltpu.VMEM((2, 2, PATCH * TOK, HD), BF16),
            pltpu.VMEM((4, 2 * TOK, HD), F32),
            pltpu.VMEM((3, Z, X, TOK, HD), BF16),
            pltpu.VMEM((3, Z, X, TOK, HD), BF16),
            pltpu.VMEM((Z, X, TOK, HD), BF16),
            pltpu.VMEM((Z, X, TOK, HD), BF16),
            pltpu.VMEM((Z, X, TOK, HD), BF16),
            pltpu.VMEM((3, X, TOK, HD), BF16),
            pltpu.VMEM((Z, X * TOK, X * Z * TOK), BF16),
            pltpu.VMEM((Z, X * TOK, 1), F32),
            pltpu.VMEM((Z, X, TOK, HD), BF16),
            pltpu.VMEM((Z, X, TOK, HD), BF16),
            pltpu.VMEM((X, TOK, HD), BF16),
            pltpu.VMEM((Z, X, TOK, HD), BF16),
            pltpu.VMEM((6, 2 * TOK, 6 * HD), BF16),
            pltpu.VMEM((4 * HD, 6 * 2 * TOK), BF16),
            pltpu.VMEM((2, PATCH * TOK, HD), F32),
            pltpu.VMEM((3, 6 * HD, 4 * HD), BF16),
            pltpu.VMEM((9, 16, 8, HD), F32),
            pltpu.VMEM((9, 8, 8, HD), F32),
            pltpu.VMEM((9, 8, 8, HD), F32),
            pltpu.VMEM((3, 9, 2, 8, HD), F32),
            pltpu.VMEM((9, 2, 8, HD), F32),
            pltpu.VMEM((n_yz, 8, HD), F32),
            pltpu.VMEM((n_yz, 8, HD), BF16),
            pltpu.VMEM((9, 2, 8, HD), BF16),
            pltpu.VMEM((9, 16, 8, HD), BF16),
            pltpu.SemaphoreType.REGULAR, dma((5,)), dma((3, 3)), dma((3, 3)), dma((3,)), dma((2,)), dma((7,)), dma((3, X)),
            dma, dma, dma((X,)), dma, dma((8, 3)), dma((2,)), dma((2,)), dma((2,)), dma((2,)),
            dma((3,)), dma((3,)), dma((3, 3)), dma((3, 3)), dma, dma, dma, dma((3,)), dma((3, 3)), dma((3, 3)), dma((3, 4)), dma((3, 4)),
        ],
        compiler_params=pltpu.CompilerParams(
            collective_id=0, has_side_effects=True, vmem_limit_bytes=60 * 1024 * 1024
        ),
        name="region_step",
    )(
        region_lengths,
        query_rows,
        key_rows,
        value_rows,
        norm_gain.reshape(HEADS, HD),
        conv_weight,
        cotangent,
    )
    return pl.pallas_call(
        results_kernel,
        out_shape=(jax.ShapeDtypeStruct((2, 4, 256, 128), BF16), jax.ShapeDtypeStruct((9, 128, 128), F32)),
        in_specs=[hbm, hbm],
        out_specs=(hbm, hbm),
        scratch_shapes=[dma((2,))],
        compiler_params=pltpu.CompilerParams(vmem_limit_bytes=2 * 1024 * 1024),
        name="results",
    )(decoded, grad.reshape(9, 128, 128))


def solution(mesh):
    placed = (
        P("seq", "dp", None),
        P("seq", "dp", None),
        P("seq", "dp", None),
        P("dp"),
        P(),
        P(),
        P("dp", "seq", None, None),
    )
    return jax.shard_map(
        body,
        mesh=mesh,
        in_specs=placed,
        out_specs=(P("dp", "seq", None, None), P()),
        check_vma=False,
    )
```
